512 devices in a mesh: ctx: 16 (over y, core), db: 4 (over z_lo), tp: 8 (over x, z_hi).
Axes of the slice: x: 4, y: 8, z: 8 (z_hi: 2, z_lo: 4; z = z_hi * 4 + z_lo), core: 2. Of those that a mesh axis runs over, the one named last changes fastest.
Arguments:
- hidden_in: bfloat16 [4, 4096, 4096], P('db', 'ctx', 'tp'), may hold values from -6 to 6
- queries: bfloat16 [4, 4096, 4096], P('db', 'ctx', 'tp')
- keys: bfloat16 [4, 4096, 4096], P('db', 'ctx', 'tp')
- values: bfloat16 [4, 4096, 4096], P('db', 'ctx', 'tp'), may hold values from -6 to 6
- cross_queries: bfloat16 [4, 4096, 4096], P('db', 'ctx', 'tp')
- neighbours: int32 [4, 64, 2], P('db', 'ctx'), may hold values from 0 to 31, as said below
- database: bfloat16 [2, 32, 128, 4096], P(None, 'db', None, 'tp')
- out_weight: bfloat16 [4096, 4096], P('tp', 'db'), may hold values from -0.125 to 0.125
Outputs:
- attended: bfloat16 [4, 4096, 4096], P('db', 'ctx', 'tp')
- mixed: bfloat16 [4, 4096, 4096], P('db', 'ctx', 'tp')
The draws below stay inside these ranges and needn't reach their ends.
Inputs may be any that keep to these rules, and one draw needn't show every extreme that they name: `neighbours`: block id n is held by database shard n // 8. Among the 8 entries of the retrieval blocks of each aligned run of 256 positions of a sequence, no shard holds more than 4, and one shard holds exactly 4; in each such run of positions this shard is the same for all sequences.
All inputs are finite; a program needn't handle non-finite values.
Results may differ from the reference program's by a relative error of at most 0.007.
Values may be sent and summed in bfloat16 or wider, within the bound.
A program may use at most 64 MiB of HBM per device.

```python
import jax
import jax.numpy as jnp
from jax import lax

D = 4096
HEADS = 32
DH = 128
TOK_DEV = 256
SPAN = 64
NEIGH = 2
NB_LEN = 128
SEQS = 4
LEN = 4096
SPANS = 64
LOOKUPS = 8
MOST = 4
DB_DEV = 8
DB_BLOCKS = 32
N_TP = 8


def pick_neighbours(key):
    base = jax.random.fold_in(key, 301)
    run_count = LEN // TOK_DEV
    hot_owner = jax.random.randint(jax.random.fold_in(base, 1), (run_count,), 0, SEQS)
    offset = jax.random.randint(jax.random.fold_in(base, 2), (SEQS, run_count, LOOKUPS), 1, SEQS)
    slot_index = jnp.arange(LOOKUPS, dtype=jnp.int32)
    owners = jnp.where(slot_index[None, None, :] < MOST, hot_owner[None, :, None], (hot_owner[None, :, None] + offset) % SEQS)
    ranking = jax.random.randint(jax.random.fold_in(base, 3), (SEQS, run_count, LOOKUPS), 0, 2 ** 20) * LOOKUPS + slot_index
    order = jnp.argsort(ranking, axis=-1)
    owners = jnp.take_along_axis(owners, order, axis=-1)
    local_ids = jax.random.randint(jax.random.fold_in(base, 4), (SEQS, run_count, LOOKUPS), 0, DB_DEV)
    return (owners * DB_DEV + local_ids).reshape(SEQS, SPANS, NEIGH).astype(jnp.int32)


def database_keys(key):
    return jax.random.normal(jax.random.fold_in(key, 201), (DB_BLOCKS, NB_LEN, D), jnp.float32)


def self_keys(key):
    return jax.random.normal(jax.random.fold_in(key, 101), (SEQS, LEN, D), jnp.float32)


def draw_neighbours(key, part):
    return pick_neighbours(key)


def draw_database(key, part):
    key_rows = database_keys(key)
    value_rows = jax.random.normal(jax.random.fold_in(key, 202), (DB_BLOCKS, NB_LEN, D), jnp.float32)
    return jnp.stack([key_rows, value_rows]).astype(jnp.bfloat16)


def draw_keys(key, part):
    base_rows = self_keys(key)
    return base_rows.astype(jnp.bfloat16)


def draw_queries(key, part):
    drawn = 2.0 * jax.random.normal(jax.random.fold_in(key, 102), (SEQS, LEN, D), jnp.float32)
    return drawn.astype(jnp.bfloat16)


def draw_cross_queries(key, part):
    drawn = 2.0 * jax.random.normal(jax.random.fold_in(key, 203), (SEQS, LEN, D), jnp.float32)
    return drawn.astype(jnp.bfloat16)


def raised(entries, own_key, source, target, blocks, factor):
    def block_of(dim):
        return (jnp.arange(entries.shape[dim]) // (entries.shape[dim] // blocks)).reshape((-1,) + (1,) * (entries.ndim - 1 - dim))

    one_side = jax.random.permutation(own_key, blocks)[block_of(target)]
    other_side = (block_of(target) + blocks // 2) % blocks
    return jnp.where((block_of(source) == one_side) | (block_of(source) == other_side), factor * entries, entries)


def levels(own_key, shape, pieces, smallest, largest):
    loudness, own = 1.0, jax.random.fold_in(own_key, 6)
    for dim, shards_of in pieces:
        steps = jnp.exp(jax.random.uniform(jax.random.fold_in(own, dim), (shards_of,), jnp.float32, smallest / len(pieces), largest / len(pieces)))
        loudness = loudness * jnp.repeat(steps, shape[dim] // shards_of).reshape([-1 if axis == dim else 1 for axis in range(len(shape))])
    return loudness


def bell_draw(own_key, dims, width, bound, shards=(), kind=jnp.bfloat16):
    result = width * jax.random.normal(own_key, dims, jnp.float32)
    if shards:
        result = result * levels(own_key, dims, shards, -0.22, 0.18)
    return jnp.clip(result, -bound, bound).astype(kind)


def gaussian_with(rng, extent, width, limit, cuts, heavy, kind=jnp.bfloat16):
    values = width * jax.random.normal(rng, extent, jnp.float32)
    if cuts:
        values = values * levels(rng, extent, cuts, -0.22, 0.18)
    return jnp.clip(raised(values, jax.random.fold_in(rng, 3), *heavy), -limit, limit).astype(kind)


def setup_inputs(seed: int = 0) -> dict:
    splits = jax.random.split(jax.random.key(seed), 9)
    hidden_in = bell_draw(splits[0], (SEQS, LEN, D), 1.0, 6.0, ((0, 4), (1, 16), (2, 8)))
    queries = draw_queries(jax.random.fold_in(splits[8], 71), 0)
    keys = draw_keys(jax.random.fold_in(splits[8], 71), 0)
    values = bell_draw(splits[3], (SEQS, LEN, D), 1.0, 6.0, ((0, 4), (1, 16), (2, 8)))
    cross_queries = draw_cross_queries(jax.random.fold_in(splits[8], 71), 0)
    neighbours = draw_neighbours(jax.random.fold_in(splits[8], 71), 0)
    database = draw_database(jax.random.fold_in(splits[8], 71), 0)
    out_weight = gaussian_with(splits[7], (D, D), D ** -0.5, 0.125, ((0, 8), (1, 4)), (0, 1, 8, 2.0))
    return dict(hidden_in=hidden_in, queries=queries, keys=keys, values=values, cross_queries=cross_queries, neighbours=neighbours, database=database, out_weight=out_weight)


def reference(hidden_in, queries, keys, values, cross_queries, neighbours, database, out_weight):
    scale = 1.0 / (DH ** 0.5)

    def by_head(array):
        return array.reshape(SEQS, LEN, HEADS, DH).transpose(0, 2, 1, 3).reshape(SEQS * HEADS, LEN, DH)

    q_all = by_head(queries)
    k_all = by_head(keys)
    v_all = by_head(values)
    position = jnp.arange(LEN, dtype=jnp.int32)
    allowed = position[None, :] <= position[:, None]

    def self_head(item):
        score = jnp.dot(q_all[item], k_all[item].T, preferred_element_type=jnp.float32) * scale
        peak = jnp.max(jnp.where(allowed, score, -1e30), axis=-1)
        weights = jnp.where(allowed, jnp.exp(score - peak[:, None]), 0.0)
        total = jnp.sum(weights, axis=-1)
        accum = jnp.dot(weights.astype(jnp.bfloat16), v_all[item], preferred_element_type=jnp.float32)
        return (accum / total[:, None]).astype(jnp.bfloat16)

    heads_out = lax.map(self_head, jnp.arange(SEQS * HEADS, dtype=jnp.int32))
    attended = heads_out.reshape(SEQS, HEADS, LEN, DH).transpose(0, 2, 1, 3).reshape(SEQS, LEN, D)

    def cross_item(item):
        seq_index = item // SPANS
        span_index = item % SPANS
        query = lax.dynamic_slice_in_dim(cross_queries[seq_index], (span_index * SPAN).astype(jnp.int32), SPAN, 0)
        block_ids = neighbours[seq_index, span_index]
        near_keys = database[0][block_ids].reshape(NEIGH * NB_LEN, HEADS, DH).astype(jnp.float32)
        near_values = database[1][block_ids].reshape(NEIGH * NB_LEN, HEADS, DH).astype(jnp.float32)
        query_heads = query.reshape(SPAN, HEADS, DH).astype(jnp.float32)
        score = jnp.einsum("qhd,khd->hqk", query_heads, near_keys) * scale
        peak = jnp.max(score, axis=-1)
        weights = jnp.exp(score - peak[..., None])
        total = jnp.sum(weights, axis=-1)
        rounded = lax.optimization_barrier(weights.astype(jnp.bfloat16)).astype(jnp.float32)
        accum = jnp.einsum("hqk,khd->qhd", rounded, near_values)
        return (accum / total.T[:, :, None]).reshape(SPAN, D).astype(jnp.bfloat16)

    cross_out = lax.map(cross_item, jnp.arange(SEQS * SPANS, dtype=jnp.int32)).reshape(SEQS * LEN, D)
    rows_block = D // N_TP
    summed = hidden_in.reshape(SEQS * LEN, D).astype(jnp.float32)
    for block in range(N_TP):
        part_sum = jnp.dot(cross_out[:, block * rows_block:(block + 1) * rows_block], out_weight[block * rows_block:(block + 1) * rows_block, :], preferred_element_type=jnp.float32)
        summed = summed + lax.optimization_barrier(part_sum.astype(jnp.bfloat16)).astype(jnp.float32)
    mixed = summed.astype(jnp.bfloat16).reshape(SEQS, LEN, D)
    return attended, mixed
```

```python
import functools
import math

import jax
import jax.numpy as jnp
from jax import lax
from jax.experimental import pallas as pl
from jax.experimental.pallas import tpu as pltpu
from jax.sharding import PartitionSpec as P

DH = 128
SPAN = 64
NEIGH = 2
SLOTS = 4
PER_SHARD = 8
ROW_BLOCKS = 2
MESH = pl.DeviceIdType.MESH
SCALE = 1.0 / math.sqrt(DH)
SCALE2 = SCALE * math.log2(math.e)
LOG2E = math.log2(math.e)
NT = (((1,), (1,)), ((), ()))


def remote(src, dst, send_sem, recv_sem, **where):
    return pltpu.make_async_remote_copy(
        src_ref=src, dst_ref=dst, send_sem=send_sem, recv_sem=recv_sem, device_id=where, device_id_type=MESH
    )


def layer(sizes, near_ref, hid_hbm, q_hbm, k_hbm, v_hbm, cq_hbm, db_hbm, w_hbm, att_ref, mixed_ref, *scratch):
    n_y, n_d, n_x = sizes
    half = n_y // 2
    (kv, qv, hid, nbv, nbs, tab, dbv, wg, osend, orecv, stf, stsend, strecv, stat, co, terms, xsend, xrecv,
     mine, zsend, zrecv, mref, lref, acc,
     loc_sem, ps, pr, ms, mr, cs, cr, qs, qr, ns, nr, nl, os_, or_, ss, sr, wzs, wzr, wps, wpr, wms, wmr, wcs, wcr,
     xs, xr, zs, zr) = scratch[n_d:]
    cqa = scratch[:n_d]
    rows = qv.shape[0]
    width = qv.shape[1]
    heads = width // DH
    spans = rows // SPAN
    entries = spans * NEIGH

    i = lax.axis_index("ctx")
    d = lax.axis_index("db")
    t = lax.axis_index("tp")
    y, c = i // 2, i % 2
    x, zh = t // 2, t % 2
    other = i + 1 - 2 * c
    up = (i + 2) % (2 * n_y)
    down = (i + 2 * n_y - 2) % (2 * n_y)
    right = ((x + 1) % n_x) * 2 + zh
    left = ((x + n_x - 1) % n_x) * 2 + zh
    across = x * 2 + 1 - zh

    loads = [
        (q_hbm, qv), (k_hbm, kv.at[i, 0]), (v_hbm, kv.at[i, 1]), (cq_hbm, cqa[0]),
        (db_hbm, dbv), (w_hbm, wg.at[:, 0]), (hid_hbm, hid),
    ]
    local = [pltpu.make_async_copy(a, b, loc_sem.at[n]) for n, (a, b) in enumerate(loads)]
    for copy in local:
        copy.start()

    lane = lax.broadcasted_iota(jnp.int32, (8, 128), 1)
    ids = jnp.zeros((8, 128), jnp.int32)
    for n in range(entries):
        ids = jnp.where(lane == n, near_ref[n // NEIGH, n % NEIGH], ids)
    nbv[0] = ids

    barrier = pltpu.get_barrier_semaphore()
    greet = [dict(ctx=up), dict(ctx=down), dict(ctx=other), dict(tp=right), dict(tp=left), dict(tp=across)]
    greet += [dict(db=(d + m) % n_d) for m in range(1, n_d)]
    for where in greet:
        pl.semaphore_signal(barrier, inc=1, device_id=where, device_id_type=MESH)
    pl.semaphore_wait(barrier, len(greet))

    def id_copy(m):
        return remote(nbv.at[0], nbv.at[n_d - m], ns.at[n_d - m], nr.at[n_d - m], db=(d + m) % n_d)

    def query_copy(m):
        return remote(cq_hbm, cqa[n_d - m], qs.at[n_d - m], qr.at[n_d - m], db=(d + m) % n_d)

    def weight_copy(m):
        j = n_d - m
        return remote(w_hbm.at[i], wg.at[i, j], wzs.at[j], wzr.at[j], db=(d + m) % n_d)

    def plus_has(step, part):
        return step < half - 1 or part == 0

    def plus_copy(step, part):
        slot = 2 * (y - step) + c
        src = (k_hbm, v_hbm)[part] if step == 0 else kv.at[slot, part]
        return remote(src, kv.at[slot, part], ps.at[step, part], pr.at[step, part], ctx=up)

    def minus_has(step, part):
        return part == 1 or step <= half - 2

    def minus_good(source, part):
        return source <= (half - 1 if part == 1 else half - 2)

    def minus_copy(step, part):
        slot = 2 * ((y + step) % n_y) + c
        src = (k_hbm, v_hbm)[part] if step == 0 else kv.at[slot, part]
        return remote(src, kv.at[slot, part], ms.at[step, part], mr.at[step, part], ctx=down)

    def pass_copy(source, part, own):
        slot = 2 * source + c
        src = (k_hbm, v_hbm)[part] if own else kv.at[slot, part]
        return remote(src, kv.at[slot, part], cs.at[source, part], cr.at[source, part], ctx=other)

    for m in range(1, n_d):
        id_copy(m).start()
    for m in range(1, n_d):
        query_copy(m).start()
    for part in (0, 1):
        if plus_has(0, part):
            pl.when(y < n_y - 1)(lambda part=part: plus_copy(0, part).start())
        if minus_has(0, part):
            pl.when(minus_good(y, part))(lambda part=part: minus_copy(0, part).start())
        pl.when(c == 0)(lambda part=part: pass_copy(y, part, True).start())
    for m in range(1, n_d):
        weight_copy(m).start()

    def attend_first():
        row = lax.broadcasted_iota(jnp.int32, (rows, rows), 0)
        col = lax.broadcasted_iota(jnp.int32, (rows, rows), 1)
        keep = col <= row
        for h in range(heads):
            hs = slice(h * DH, (h + 1) * DH)
            s = lax.dot_general(qv[:, hs], kv[i, 0, :, hs], NT, preferred_element_type=jnp.float32)
            s = jnp.where(keep, s, -1e30)
            peak = jnp.max(s, axis=-1, keepdims=True)
            p = jnp.exp2((s - peak) * SCALE2)
            mref[h] = peak
            lref[h] = jnp.sum(p, axis=-1, keepdims=True)
            acc[h] = jnp.dot(p.astype(jnp.bfloat16), kv[i, 1, :, hs], preferred_element_type=jnp.float32)

    def attend(start, count):
        for h in range(heads):
            hs = slice(h * DH, (h + 1) * DH)
            keys = kv[pl.ds(start, count), 0, :, hs].reshape(count * rows, DH)
            vals = kv[pl.ds(start, count), 1, :, hs].reshape(count * rows, DH)
            s = lax.dot_general(qv[:, hs], keys, NT, preferred_element_type=jnp.float32)
            before = mref[h]
            peak = jnp.maximum(before, jnp.max(s, axis=-1, keepdims=True))
            p = jnp.exp2((s - peak) * SCALE2)
            factor = jnp.exp2((before - peak) * SCALE2)
            mref[h] = peak
            lref[h] = lref[h] * factor + jnp.sum(p, axis=-1, keepdims=True)
            acc[h] = acc[h] * factor + jnp.dot(p.astype(jnp.bfloat16), vals, preferred_element_type=jnp.float32)

    def wait_passed(source):
        for part in (0, 1):
            slot = 2 * source + 1 - c
            remote(
                kv.at[slot, part], kv.at[slot, part], cs.at[source, part], cr.at[source, part], ctx=other
            ).wait_recv()

    def attend_pair(source):
        wait_passed(source)
        attend(2 * source, 2)

    def move_step(step):
        for part in (0, 1):
            if plus_has(step, part):
                source = y - 1 - step

                @pl.when(source >= 0)
                def _():
                    slot = 2 * source + c
                    remote(
                        kv.at[slot, part], kv.at[slot, part], ps.at[step, part], pr.at[step, part], ctx=up
                    ).wait_recv()
                    if step + 1 < half and plus_has(step + 1, part):
                        pl.when(y < n_y - 1)(lambda: plus_copy(step + 1, part).start())
                    pass_copy(source, part, False).start()

            if minus_has(step, part):
                source2 = (y + 1 + step) % n_y

                @pl.when(minus_good(source2, part))
                def _():
                    slot = 2 * source2 + c
                    remote(
                        kv.at[slot, part], kv.at[slot, part], ms.at[step, part], mr.at[step, part], ctx=down
                    ).wait_recv()
                    if step + 1 < half and minus_has(step + 1, part):
                        minus_copy(step + 1, part).start()
                    pl.when(source2 < y)(lambda: pass_copy(source2, part, False).start())

    def attend_step(step):
        if step < half - 1:
            pl.when(y - 1 - step >= 0)(lambda: attend_pair(y - 1 - step))
            pl.when(y + 1 + step >= n_y)(lambda: attend_pair(y + 1 + step - n_y))
        else:
            pl.when(y >= half)(lambda: attend_pair(y - half))

    def wplus(step):
        slot = 2 * ((y - step + n_y) % n_y) + c
        piece = wg.at[slot, pl.ds(1, n_d - 1)]
        return remote(piece, piece, wps.at[step], wpr.at[step], ctx=up)

    def wminus(step):
        slot = 2 * ((y + step) % n_y) + c
        piece = wg.at[slot, pl.ds(1, n_d - 1)]
        return remote(piece, piece, wms.at[step], wmr.at[step], ctx=down)

    def wpass(source):
        piece = wg.at[2 * source + c, pl.ds(1, n_d - 1)]
        return remote(piece, piece, wcs.at[source], wcr.at[source], ctx=other)

    def weight_step(step):
        if step == 0:
            for j in range(1, n_d):
                remote(w_hbm.at[i], wg.at[i, j], wzs.at[j], wzr.at[j], db=d).wait_recv()
            source = y
        else:
            source = (y - step + n_y) % n_y
            piece = wg.at[2 * source + c, pl.ds(1, n_d - 1)]
            remote(piece, piece, wps.at[step - 1], wpr.at[step - 1], ctx=up).wait_recv()
        if step < half:
            wplus(step).start()
        wpass(source).start()
        if step < half - 1 and step == 0:
            wminus(0).start()
        if 1 <= step <= half - 1:
            source2 = (y + step) % n_y
            piece2 = wg.at[2 * source2 + c, pl.ds(1, n_d - 1)]
            remote(piece2, piece2, wms.at[step - 1], wmr.at[step - 1], ctx=down).wait_recv()
            if step < half - 1:
                wminus(step).start()
            wpass(source2).start()

    def weight_ready():
        for source in range(n_y):
            piece = wg.at[2 * source + 1 - c, pl.ds(1, n_d - 1)]
            remote(piece, piece, wcs.at[source], wcr.at[source], ctx=other).wait_recv()

    def serve(j):
        if j > 0:
            remote(nbv.at[0], nbv.at[j], ns.at[j], nr.at[j], db=d).wait_recv()
        move = pltpu.make_async_copy(nbv.at[j], nbs.at[j], nl.at[j])
        move.start()
        move.wait()
        spots = [jnp.int32(0)] * SLOTS
        blocks = [jnp.int32(0)] * SLOTS
        seen = jnp.int32(0)
        for n in range(entries):
            block = nbs[j, 0, n]
            hit = (block // PER_SHARD) == d
            for k in range(SLOTS):
                take = jnp.logical_and(hit, seen == k)
                spots[k] = jnp.where(take, n // NEIGH, spots[k])
                blocks[k] = jnp.where(take, block % PER_SHARD, blocks[k])
            seen = seen + jnp.where(hit, 1, 0)
        for k in range(SLOTS):
            tab[0, k] = spots[k]
            tab[1, k] = blocks[k]
        if j > 0:
            remote(cq_hbm, cqa[j], qs.at[j], qr.at[j], db=d).wait_recv()

        def one(k, carry):
            query = cqa[j][tab[0, k]]
            keys = dbv[0, tab[1, k]]
            vals = dbv[1, tab[1, k]]
            lanes = lax.broadcasted_iota(jnp.int32, (SPAN, 128), 1)
            st = jnp.zeros((SPAN, 128), jnp.float32)
            for h in range(heads):
                hs = slice(h * DH, (h + 1) * DH)
                s = lax.dot_general(query[:, hs], keys[:, hs], NT, preferred_element_type=jnp.float32)
                peak = jnp.max(s, axis=-1, keepdims=True)
                p = jnp.exp2((s - peak) * SCALE2)
                total = jnp.sum(p, axis=-1, keepdims=True)
                o = jnp.dot(p.astype(jnp.bfloat16), vals[:, hs], preferred_element_type=jnp.float32) / total
                if j == 0:
                    orecv[0, k, :, hs] = o.astype(jnp.bfloat16)
                else:
                    osend[j - 1, k, :, hs] = o.astype(jnp.bfloat16)
                st = jnp.where(lanes == h, peak * SCALE + jnp.log(total), st)
            if j == 0:
                stat[0, k] = st
            else:
                stf[k] = st
            return carry

        lax.fori_loop(0, SLOTS, one, 0)
        if j > 0:
            stsend[j - 1] = stf[...].reshape(SLOTS * SPAN, 128).T[:8]
            out_copy(j).start()
            stat_copy(j).start()

    def out_copy(j):
        return remote(osend.at[j - 1], orecv.at[n_d - j], os_.at[n_d - j], or_.at[n_d - j], db=(d + j) % n_d)

    def stat_copy(j):
        return remote(stsend.at[j - 1], strecv.at[n_d - j], ss.at[n_d - j], sr.at[n_d - j], db=(d + j) % n_d)

    def collect(j):
        remote(osend.at[0], orecv.at[j], os_.at[j], or_.at[j], db=d).wait_recv()
        remote(stsend.at[0], strecv.at[j], ss.at[j], sr.at[j], db=d).wait_recv()
        wide = jnp.concatenate([strecv[j]] * 16, axis=0)
        stat[j] = wide.T.reshape(SLOTS, SPAN, 128)

    def combine():
        places = []
        owners = []
        for n in range(entries):
            owner = nbs[0, 0, n] // PER_SHARD
            rank = jnp.int32(0)
            for earlier in owners:
                rank = rank + jnp.where(earlier == owner, 1, 0)
            owners.append(owner)
            places.append(((owner - d + n_d) % n_d, jnp.minimum(rank, SLOTS - 1)))
        for u in range(spans):
            (oa, ka), (ob, kb) = places[2 * u], places[2 * u + 1]
            sa, sb = stat[oa, ka], stat[ob, kb]
            peak = jnp.maximum(sa, sb)
            ea = jnp.exp2((sa - peak) * LOG2E)
            eb = jnp.exp2((sb - peak) * LOG2E)
            inv = 1.0 / (ea + eb)
            ea, eb = ea * inv, eb * inv
            va, vb = orecv[oa, ka], orecv[ob, kb]
            for h in range(heads):
                hs = slice(h * DH, (h + 1) * DH)
                o = va[:, hs].astype(jnp.float32) * ea[:, h:h + 1] + vb[:, hs].astype(jnp.float32) * eb[:, h:h + 1]
                co[u * SPAN:(u + 1) * SPAN, hs] = o.astype(jnp.bfloat16)

    half_w = terms.shape[2]

    def project(rho, side):
        j = ((x + rho) % n_x - d + n_d) % n_d
        block = wg[:, j, :, side * half_w:(side + 1) * half_w].reshape(width, half_w)
        return jnp.dot(co[...], block, preferred_element_type=jnp.float32)

    rb_rows = rows // ROW_BLOCKS

    def ring_copy(side, step, rb):
        rs = pl.ds(rb * rb_rows, rb_rows)
        return remote(
            xsend.at[side, step, rs], xrecv.at[side, step, rs], xs.at[side, step, rb], xr.at[side, step, rb],
            tp=(right, left)[side],
        )

    def rho_of(side, step):
        return (n_x - 1 - step) % n_x if side == 0 else (1 + step) % n_x

    def ring_start():
        for side in (0, 1):
            xsend[side, 0] = project(rho_of(side, 0), side).astype(jnp.bfloat16)
            for rb in range(ROW_BLOCKS):
                ring_copy(side, 0, rb).start()
        for step in range(1, n_x):
            for side in (0, 1):
                terms[side * (n_x - 1) + step - 1] = project(rho_of(side, step), side)

    def ring_step(step):
        for rb in range(ROW_BLOCKS):
            rs = slice(rb * rb_rows, (rb + 1) * rb_rows)
            for side in (0, 1):
                ring_copy(side, step - 1, rb).wait_recv()
                total = xrecv[side, step - 1, rs].astype(jnp.float32) + terms[side * (n_x - 1) + step - 1, rs]
                xsend[side, step, rs] = total.astype(jnp.bfloat16)
                ring_copy(side, step, rb).start()

    def z_copy(rb):
        rs = pl.ds(rb * rb_rows, rb_rows)
        return remote(zsend.at[rs], zrecv.at[rs], zs.at[rb], zr.at[rb], tp=across)

    def ring_end():
        for rb in range(ROW_BLOCKS):
            rs = slice(rb * rb_rows, (rb + 1) * rb_rows)
            sums = []
            for side in (0, 1):
                ring_copy(side, n_x - 2, rb).wait_recv()
                sums.append(
                    xrecv[side, n_x - 2, rs].astype(jnp.float32) + terms[side * (n_x - 1) + n_x - 2, rs]
                )
            zsend[rs] = jnp.where(zh == 0, sums[1], sums[0]).astype(jnp.bfloat16)
            z_copy(rb).start()
            mine[rs] = jnp.where(zh == 0, sums[0], sums[1]) + hid[rs].astype(jnp.float32)

    def finish_self():
        for h in range(heads):
            hs = slice(h * DH, (h + 1) * DH)
            att_ref[:, hs] = (acc[h] / lref[h]).astype(jnp.bfloat16)

    for n in (3, 4):
        local[n].wait()
    serve(0)
    for n in (0, 1, 2):
        local[n].wait()
    attend_first()
    move_step(0)

    @pl.when(c == 1)
    def _():
        wait_passed(y)
        attend(i - 1, 1)

    for j in [v for v in (1, n_d - 1) if v < n_d]:
        if j == 1 or n_d > 2:
            serve(j)
    for j in range(2, n_d - 1):
        serve(j)
    weight_step(0)
    move_step(1) if half > 1 else None
    weight_step(1)
    attend_step(0)
    weight_step(2) if half >= 2 else None
    move_step(2) if half > 2 else None
    if half > 1:
        attend_step(1)
    for step in range(3, half + 1):
        weight_step(step)
    for j in range(1, n_d):
        collect(j)
    combine()
    weight_ready()
    local[5].wait()
    ring_start()
    if half > 3:
        move_step(3)
    for step in range(1, n_x - 1):
        ring_step(step)
        if step == 1 and half > 2:
            attend_step(2)
    local[6].wait()
    ring_end()
    if half > 3:
        attend_step(3)
    finish_self()
    for rb in range(ROW_BLOCKS):
        rs = slice(rb * rb_rows, (rb + 1) * rb_rows)
        z_copy(rb).wait_recv()
        mixed_ref[rs] = (mine[rs] + zrecv[rs].astype(jnp.float32)).astype(jnp.bfloat16)

    for m in range(1, n_d):
        id_copy(m).wait_send()
        query_copy(m).wait_send()
        weight_copy(m).wait_send()
        out_copy(m).wait_send()
        stat_copy(m).wait_send()
    for step in range(half):
        for part in (0, 1):
            if plus_has(step, part):
                pl.when(jnp.logical_and(y - step >= 0, y < n_y - 1))(
                    lambda step=step, part=part: plus_copy(step, part).wait_send())
            if minus_has(step, part):
                pl.when(minus_good((y + step) % n_y, part))(
                    lambda step=step, part=part: minus_copy(step, part).wait_send())
        wplus(step).wait_send()
        if step < half - 1:
            wminus(step).wait_send()
    for source in range(n_y):
        for part in (0, 1):
            pl.when(source < y)(lambda source=source, part=part: pass_copy(source, part, False).wait_send())
        wpass(source).wait_send()
    for part in (0, 1):
        pl.when(c == 0)(lambda part=part: pass_copy(y, part, True).wait_send())
    for side in (0, 1):
        for step in range(n_x - 1):
            for rb in range(ROW_BLOCKS):
                ring_copy(side, step, rb).wait_send()
    for rb in range(ROW_BLOCKS):
        z_copy(rb).wait_send()


def shards(sizes, hidden_in, queries, keys, values, cross_queries, neighbours, database, out_weight):
    n_y, n_d, n_x = sizes
    half = n_y // 2
    rows, width = queries.shape[1:]
    heads = width // DH
    spans = rows // SPAN
    n_c = 2 * n_y
    piece = width // n_c
    cols = out_weight.shape[1]
    half_w = cols // 2
    bf16, f32 = jnp.bfloat16, jnp.float32
    vm, dma = pltpu.VMEM, pltpu.SemaphoreType.DMA
    any_spec = pl.BlockSpec(memory_space=pl.ANY)
    scratch = [vm((spans, SPAN, width), bf16) for _ in range(n_d)] + [
        vm((n_c, 2, rows, width), bf16),
        vm((rows, width), bf16),
        vm((rows, width), bf16),
        vm((n_d, 8, 128), jnp.int32),
        pltpu.SMEM((n_d, 8, 128), jnp.int32),
        pltpu.SMEM((2, SLOTS), jnp.int32),
        vm(database.shape, bf16),
        vm((n_c, n_d, piece, cols), bf16),
        vm((max(n_d - 1, 1), SLOTS, SPAN, width), bf16),
        vm((n_d, SLOTS, SPAN, width), bf16),
        vm((SLOTS, SPAN, 128), f32),
        vm((max(n_d - 1, 1), 8, SLOTS * SPAN), f32),
        vm((n_d, 8, SLOTS * SPAN), f32),
        vm((n_d, SLOTS, SPAN, 128), f32),
        vm((rows, width), bf16),
        vm((2 * (n_x - 1), rows, half_w), f32),
        vm((2, n_x - 1, rows, half_w), bf16),
        vm((2, n_x - 1, rows, half_w), bf16),
        vm((rows, half_w), f32),
        vm((rows, half_w), bf16),
        vm((rows, half_w), bf16),
        vm((heads, rows, 1), f32),
        vm((heads, rows, 1), f32),
        vm((heads, rows, DH), f32),
        dma((7,)),
        dma((half, 2)), dma((half, 2)), dma((half, 2)), dma((half, 2)),
        dma((n_y, 2)), dma((n_y, 2)),
        dma((n_d,)), dma((n_d,)), dma((n_d,)), dma((n_d,)), dma((n_d,)),
        dma((n_d,)), dma((n_d,)), dma((n_d,)), dma((n_d,)),
        dma((n_d,)), dma((n_d,)),
        dma((half,)), dma((half,)), dma((half,)), dma((half,)),
        dma((n_y,)), dma((n_y,)),
        dma((2, n_x - 1, ROW_BLOCKS)), dma((2, n_x - 1, ROW_BLOCKS)),
        dma((ROW_BLOCKS,)), dma((ROW_BLOCKS,)),
    ]
    attended, mixed = pl.pallas_call(
        functools.partial(layer, sizes),
        out_shape=(
            jax.ShapeDtypeStruct((rows, width), bf16),
            jax.ShapeDtypeStruct((rows, half_w), bf16),
        ),
        in_specs=[pl.BlockSpec(memory_space=pltpu.SMEM)] + [any_spec] * 7,
        out_specs=(pl.BlockSpec(memory_space=pltpu.VMEM), pl.BlockSpec(memory_space=pltpu.VMEM)),
        scratch_shapes=scratch,
        compiler_params=pltpu.CompilerParams(
            collective_id=0, has_side_effects=True, vmem_limit_bytes=56 * 1024 * 1024
        ),
        name="layer",
    )(
        neighbours[0],
        hidden_in[0],
        queries[0],
        keys[0],
        values[0],
        cross_queries[0].reshape(spans, SPAN, width),
        database,
        out_weight.reshape(n_c, piece, cols),
    )
    return attended[None], mixed[None]


def solution(mesh):
    sizes = (mesh.shape["ctx"] // 2, mesh.shape["db"], mesh.shape["tp"] // 2)
    in_specs = (
        P("db", "ctx", "tp"),
        P("db", "ctx", "tp"),
        P("db", "ctx", "tp"),
        P("db", "ctx", "tp"),
        P("db", "ctx", "tp"),
        P("db", "ctx", None),
        P(None, "db", None, "tp"),
        P("tp", "db"),
    )
    out_specs = (P("db", "ctx", "tp"), P("db", "ctx", "tp"))
    return jax.shard_map(
        functools.partial(shards, sizes), mesh=mesh, in_specs=in_specs, out_specs=out_specs, check_vma=False
    )
```

```python
import functools
import math

import jax
import jax.numpy as jnp
from jax import lax
from jax.experimental import pallas as pl
from jax.experimental.pallas import tpu as pltpu
from jax.sharding import PartitionSpec as P

DH = 128
SPAN = 64
NEIGH = 2
SLOTS = 4
PER_SHARD = 8
ROW_BLOCKS = 2
MESH = pl.DeviceIdType.MESH
SCALE = 1.0 / math.sqrt(DH)
SCALE2 = SCALE * math.log2(math.e)
LOG2E = math.log2(math.e)
NT = (((1,), (1,)), ((), ()))


def remote(src, dst, send_sem, recv_sem, **where):
    return pltpu.make_async_remote_copy(
        src_ref=src, dst_ref=dst, send_sem=send_sem, recv_sem=recv_sem, device_id=where, device_id_type=MESH
    )


def layer(sizes, near_hbm, hid_hbm, q_hbm, k_hbm, v_hbm, cq_hbm, db_hbm, w_hbm, att_ref, mixed_ref, *scratch):
    n_y, n_d, n_x = sizes
    half = n_y // 2
    (kv, qv, hid, near_ref, nbv, nbs, dbv, wg, osend, orecv, stsend, strecv, stat, co, terms, xsend, xrecv,
     mine, zsend, zrecv, mref, lref, acc,
     loc_sem, ps, pr, ms, mr, cs, cr, qs, qr, ns, nr, nl, os_, or_, ss, sr, wzs, wzr, wps, wpr, wms, wmr, wcs, wcr,
     xs, xr, zs, zr) = scratch[n_d:]
    cqa = scratch[:n_d]
    rows = qv.shape[0]
    width = qv.shape[1]
    heads = width // DH
    spans = rows // SPAN
    entries = spans * NEIGH

    i = lax.axis_index("ctx")
    d = lax.axis_index("db")
    t = lax.axis_index("tp")
    y, c = i // 2, i % 2
    x, zh = t // 2, t % 2
    other = i + 1 - 2 * c
    up = (i + 2) % (2 * n_y)
    down = (i + 2 * n_y - 2) % (2 * n_y)
    right = ((x + 1) % n_x) * 2 + zh
    left = ((x + n_x - 1) % n_x) * 2 + zh
    across = x * 2 + 1 - zh

    loads = [
        (q_hbm, qv), (k_hbm, kv.at[i, 0]), (v_hbm, kv.at[i, 1]), (cq_hbm, cqa[0]),
        (db_hbm, dbv), (w_hbm, wg.at[:, 0]), (hid_hbm, hid), (near_hbm.at[0], near_ref),
    ]
    local = [pltpu.make_async_copy(a, b, loc_sem.at[n]) for n, (a, b) in enumerate(loads)]
    for n in (7, 3, 4, 0, 1, 2, 5, 6):
        local[n].start()
    barrier = pltpu.get_barrier_semaphore()
    greet = [dict(ctx=up), dict(ctx=down), dict(ctx=other), dict(tp=right), dict(tp=left), dict(tp=across)]
    greet += [dict(db=(d + m) % n_d) for m in range(1, n_d)]
    for where in greet:
        pl.semaphore_signal(barrier, inc=1, device_id=where, device_id_type=MESH)

    local[7].wait()
    lane = lax.broadcasted_iota(jnp.int32, (8, 128), 1)
    ids = jnp.zeros((8, 128), jnp.int32)
    for n in range(entries):
        ids = jnp.where(lane == n, near_ref[n // NEIGH, n % NEIGH], ids)
    nbv[0] = ids
    pl.semaphore_wait(barrier, len(greet))

    def id_copy(m):
        return remote(nbv.at[0], nbv.at[n_d - m], ns.at[n_d - m], nr.at[n_d - m], db=(d + m) % n_d)

    def query_copy(m):
        return remote(cq_hbm, cqa[n_d - m], qs.at[n_d - m], qr.at[n_d - m], db=(d + m) % n_d)

    def weight_copy(m):
        j = n_d - m
        return remote(w_hbm.at[i], wg.at[i, j], wzs.at[j], wzr.at[j], db=(d + m) % n_d)

    def plus_has(step, part):
        return step < half - 1 or part == 0

    def plus_copy(step, part):
        slot = 2 * (y - step) + c
        src = (k_hbm, v_hbm)[part] if step == 0 else kv.at[slot, part]
        return remote(src, kv.at[slot, part], ps.at[step, part], pr.at[step, part], ctx=up)

    def minus_has(step, part):
        return part == 1 or step <= half - 2

    def minus_good(source, part):
        return source <= (half - 1 if part == 1 else half - 2)

    def minus_copy(step, part):
        slot = 2 * ((y + step) % n_y) + c
        src = (k_hbm, v_hbm)[part] if step == 0 else kv.at[slot, part]
        return remote(src, kv.at[slot, part], ms.at[step, part], mr.at[step, part], ctx=down)

    def pass_copy(source, part, own):
        slot = 2 * source + c
        src = (k_hbm, v_hbm)[part] if own else kv.at[slot, part]
        return remote(src, kv.at[slot, part], cs.at[source, part], cr.at[source, part], ctx=other)

    def kv_start(part):
        pl.when(y < n_y - 1)(lambda: plus_copy(0, part).start())
        pl.when(minus_good(y, part))(lambda: minus_copy(0, part).start())
        pl.when(c == 0)(lambda: pass_copy(y, part, True).start())

    for m in range(1, n_d):
        id_copy(m).start()
    for m in range(1, n_d):
        weight_copy(m).start()
    for m in range(1, n_d):
        query_copy(m).start()
    kv_start(0)

    def attend_first():
        row = lax.broadcasted_iota(jnp.int32, (rows, rows), 0)
        col = lax.broadcasted_iota(jnp.int32, (rows, rows), 1)
        keep = col <= row
        for h in range(heads):
            hs = slice(h * DH, (h + 1) * DH)
            s = lax.dot_general(qv[:, hs], kv[i, 0, :, hs], NT, preferred_element_type=jnp.float32)
            s = jnp.where(keep, s, -1e30)
            peak = jnp.max(s, axis=-1, keepdims=True)
            p = jnp.exp2((s - peak) * SCALE2)
            mref[h] = peak
            lref[h] = jnp.sum(p, axis=-1, keepdims=True)
            acc[h] = jnp.dot(p.astype(jnp.bfloat16), kv[i, 1, :, hs], preferred_element_type=jnp.float32)

    def attend(start, count):
        for h in range(heads):
            hs = slice(h * DH, (h + 1) * DH)
            keys = kv[pl.ds(start, count), 0, :, hs].reshape(count * rows, DH)
            vals = kv[pl.ds(start, count), 1, :, hs].reshape(count * rows, DH)
            s = lax.dot_general(qv[:, hs], keys, NT, preferred_element_type=jnp.float32)
            before = mref[h]
            peak = jnp.maximum(before, jnp.max(s, axis=-1, keepdims=True))
            p = jnp.exp2((s - peak) * SCALE2)
            factor = jnp.exp2((before - peak) * SCALE2)
            mref[h] = peak
            lref[h] = lref[h] * factor + jnp.sum(p, axis=-1, keepdims=True)
            acc[h] = acc[h] * factor + jnp.dot(p.astype(jnp.bfloat16), vals, preferred_element_type=jnp.float32)

    def wait_passed(source):
        for part in (0, 1):
            slot = 2 * source + 1 - c
            remote(
                kv.at[slot, part], kv.at[slot, part], cs.at[source, part], cr.at[source, part], ctx=other
            ).wait_recv()

    def attend_pair(source):
        wait_passed(source)
        attend(2 * source, 2)

    def advance(step, *parts):
        for part in parts:
            if plus_has(step, part):
                source = y - 1 - step

                @pl.when(source >= 0)
                def _():
                    slot = 2 * source + c
                    remote(
                        kv.at[slot, part], kv.at[slot, part], ps.at[step, part], pr.at[step, part], ctx=up
                    ).wait_recv()
                    if step + 1 < half and plus_has(step + 1, part):
                        pl.when(y < n_y - 1)(lambda: plus_copy(step + 1, part).start())
                    pass_copy(source, part, False).start()

            if minus_has(step, part):
                source2 = (y + 1 + step) % n_y

                @pl.when(minus_good(source2, part))
                def _():
                    slot = 2 * source2 + c
                    remote(
                        kv.at[slot, part], kv.at[slot, part], ms.at[step, part], mr.at[step, part], ctx=down
                    ).wait_recv()
                    if step + 1 < half and minus_has(step + 1, part):
                        minus_copy(step + 1, part).start()
                    pl.when(source2 < y)(lambda: pass_copy(source2, part, False).start())

    def attend_step(step):
        if step < half - 1:
            pl.when(y - 1 - step >= 0)(lambda: attend_pair(y - 1 - step))
            pl.when(y + 1 + step >= n_y)(lambda: attend_pair(y + 1 + step - n_y))
        else:
            pl.when(y >= half)(lambda: attend_pair(y - half))

    def wplus(step):
        slot = 2 * ((y - step + n_y) % n_y) + c
        piece = wg.at[slot, pl.ds(1, n_d - 1)]
        return remote(piece, piece, wps.at[step], wpr.at[step], ctx=up)

    def wminus(step):
        slot = 2 * ((y + step) % n_y) + c
        piece = wg.at[slot, pl.ds(1, n_d - 1)]
        return remote(piece, piece, wms.at[step], wmr.at[step], ctx=down)

    def wpass(source):
        piece = wg.at[2 * source + c, pl.ds(1, n_d - 1)]
        return remote(piece, piece, wcs.at[source], wcr.at[source], ctx=other)

    def weight_step(step):
        if step == 0:
            for j in range(1, n_d):
                remote(w_hbm.at[i], wg.at[i, j], wzs.at[j], wzr.at[j], db=d).wait_recv()
            source = y
        else:
            source = (y - step + n_y) % n_y
            piece = wg.at[2 * source + c, pl.ds(1, n_d - 1)]
            remote(piece, piece, wps.at[step - 1], wpr.at[step - 1], ctx=up).wait_recv()
        if step < half:
            wplus(step).start()
        wpass(source).start()
        if step < half - 1 and step == 0:
            wminus(0).start()
        if 1 <= step <= half - 1:
            source2 = (y + step) % n_y
            piece2 = wg.at[2 * source2 + c, pl.ds(1, n_d - 1)]
            remote(piece2, piece2, wms.at[step - 1], wmr.at[step - 1], ctx=down).wait_recv()
            if step < half - 1:
                wminus(step).start()
            wpass(source2).start()

    def weight_ready():
        for source in range(n_y):
            piece = wg.at[2 * source + 1 - c, pl.ds(1, n_d - 1)]
            remote(piece, piece, wcs.at[source], wcr.at[source], ctx=other).wait_recv()

    def id_move(j):
        return pltpu.make_async_copy(nbv.at[j], nbs.at[j], nl.at[j])

    def block_id(j, n):
        return near_ref[n // NEIGH, n % NEIGH] if j == 0 else nbs[j, 0, n]

    def lookups(j):
        spots = [jnp.int32(0)] * SLOTS
        blocks = [jnp.int32(0)] * SLOTS
        seen = jnp.int32(0)
        for n in range(entries):
            block = block_id(j, n)
            hit = (block // PER_SHARD) == d
            for k in range(min(n + 1, SLOTS)):
                take = jnp.logical_and(hit, seen == k)
                spots[k] = jnp.where(take, n // NEIGH, spots[k])
                blocks[k] = jnp.where(take, block % PER_SHARD, blocks[k])
            seen = seen + jnp.where(hit, 1, 0)
        return spots, blocks

    def serve(j, found):
        spots, blocks = found
        if j > 0:
            remote(cq_hbm, cqa[j], qs.at[j], qr.at[j], db=d).wait_recv()
        lanes = lax.broadcasted_iota(jnp.int32, (SPAN, 128), 1)
        st = jnp.zeros((SPAN, 128), jnp.float32)
        out = orecv.at[0] if j == 0 else osend.at[j - 1]
        for k in range(SLOTS):
            query = cqa[j][spots[k]]
            keys = dbv[0, blocks[k]]
            vals = dbv[1, blocks[k]]
            for h in range(heads):
                hs = slice(h * DH, (h + 1) * DH)
                s = lax.dot_general(query[:, hs], keys[:, hs], NT, preferred_element_type=jnp.float32)
                peak = jnp.max(s, axis=-1, keepdims=True)
                p = jnp.exp2((s - peak) * SCALE2)
                total = jnp.sum(p, axis=-1, keepdims=True)
                o = jnp.dot(p.astype(jnp.bfloat16), vals[:, hs], preferred_element_type=jnp.float32) * (1.0 / total)
                out[k, :, hs] = o.astype(jnp.bfloat16)
                st = jnp.where(lanes == k * heads + h, peak * SCALE2 + jnp.log(total) * LOG2E, st)
        if j == 0:
            strecv[0] = st
        else:
            stsend[j - 1] = st
            out_copy(j).start()
            stat_copy(j).start()

    def out_copy(j):
        return remote(osend.at[j - 1], orecv.at[n_d - j], os_.at[n_d - j], or_.at[n_d - j], db=(d + j) % n_d)

    def stat_copy(j):
        return remote(stsend.at[j - 1], strecv.at[n_d - j], ss.at[n_d - j], sr.at[n_d - j], db=(d + j) % n_d)

    def collect(j):
        if j > 0:
            remote(osend.at[0], orecv.at[j], os_.at[j], or_.at[j], db=d).wait_recv()
            remote(stsend.at[0], strecv.at[j], ss.at[j], sr.at[j], db=d).wait_recv()
        packed = strecv[j]
        stat[j, 0] = packed
        for k in range(1, SLOTS):
            stat[j, k] = pltpu.roll(packed, 128 - k * heads, 1)

    def combine():
        places = []
        owners = []
        for n in range(entries):
            owner = block_id(0, n) // PER_SHARD
            rank = jnp.int32(0)
            for earlier in owners:
                rank = rank + jnp.where(earlier == owner, 1, 0)
            owners.append(owner)
            places.append(((owner - d + n_d) % n_d, jnp.minimum(rank, SLOTS - 1)))
        for u in range(spans):
            (oa, ka), (ob, kb) = places[2 * u], places[2 * u + 1]
            sa, sb = stat[oa, ka], stat[ob, kb]
            peak = jnp.maximum(sa, sb)
            ea = jnp.exp2(sa - peak)
            eb = jnp.exp2(sb - peak)
            inv = 1.0 / (ea + eb)
            ea, eb = ea * inv, eb * inv
            va, vb = orecv[oa, ka], orecv[ob, kb]
            for h in range(heads):
                hs = slice(h * DH, (h + 1) * DH)
                o = va[:, hs].astype(jnp.float32) * ea[:, h:h + 1] + vb[:, hs].astype(jnp.float32) * eb[:, h:h + 1]
                co[u * SPAN:(u + 1) * SPAN, hs] = o.astype(jnp.bfloat16)

    half_w = terms.shape[2]

    def project(rho, side):
        j = ((x + rho) % n_x - d + n_d) % n_d
        block = wg[:, j, :, side * half_w:(side + 1) * half_w].reshape(width, half_w)
        return jnp.dot(co[...], block, preferred_element_type=jnp.float32)

    rb_rows = rows // ROW_BLOCKS

    def ring_copy(side, step, rb):
        rs = pl.ds(rb * rb_rows, rb_rows)
        return remote(
            xsend.at[side, step, rs], xrecv.at[side, step, rs], xs.at[side, step, rb], xr.at[side, step, rb],
            tp=(right, left)[side],
        )

    def rho_of(side, step):
        return (n_x - 1 - step) % n_x if side == 0 else (1 + step) % n_x

    def ring_start():
        for side in (0, 1):
            xsend[side, 0] = project(rho_of(side, 0), side).astype(jnp.bfloat16)
            for rb in range(ROW_BLOCKS):
                ring_copy(side, 0, rb).start()
        for step in range(1, n_x):
            for side in (0, 1):
                terms[side * (n_x - 1) + step - 1] = project(rho_of(side, step), side)

    def ring_step(step):
        for rb in range(ROW_BLOCKS):
            rs = slice(rb * rb_rows, (rb + 1) * rb_rows)
            for side in (0, 1):
                ring_copy(side, step - 1, rb).wait_recv()
                total = xrecv[side, step - 1, rs].astype(jnp.float32) + terms[side * (n_x - 1) + step - 1, rs]
                xsend[side, step, rs] = total.astype(jnp.bfloat16)
                ring_copy(side, step, rb).start()

    def z_copy(rb):
        rs = pl.ds(rb * rb_rows, rb_rows)
        return remote(zsend.at[rs], zrecv.at[rs], zs.at[rb], zr.at[rb], tp=across)

    def ring_end():
        for rb in range(ROW_BLOCKS):
            rs = slice(rb * rb_rows, (rb + 1) * rb_rows)
            sums = []
            for side in (0, 1):
                ring_copy(side, n_x - 2, rb).wait_recv()
                sums.append(
                    xrecv[side, n_x - 2, rs].astype(jnp.float32) + terms[side * (n_x - 1) + n_x - 2, rs]
                )
            zsend[rs] = jnp.where(zh == 0, sums[1], sums[0]).astype(jnp.bfloat16)
            z_copy(rb).start()
            mine[rs] = jnp.where(zh == 0, sums[0], sums[1]) + hid[rs].astype(jnp.float32)

    def finish_self():
        for h in range(heads):
            hs = slice(h * DH, (h + 1) * DH)
            att_ref[:, hs] = (acc[h] / lref[h]).astype(jnp.bfloat16)

    for n in (3, 4):
        local[n].wait()
    serve(0, lookups(0))
    for n in (0, 1, 2):
        local[n].wait()
    attend_first()
    for j in range(1, n_d):
        remote(nbv.at[0], nbv.at[j], ns.at[j], nr.at[j], db=d).wait_recv()
        id_move(j).start()
    weight_step(0)
    kv_start(1)
    found = {}
    for j in range(1, n_d):
        id_move(j).wait()
        found[j] = lookups(j)
    collect(0)
    weight_step(1)
    serve(1, found[1])
    weight_step(2)
    advance(0, 0)
    serve(3, found[3])
    weight_step(3)
    serve(2, found[2])
    weight_step(4)
    advance(0, 1)
    pl.when(c == 1)(lambda: wait_passed(y))
    pl.when(c == 1)(lambda: attend(i - 1, 1))
    attend_step(0)
    advance(1, 0, 1)
    attend_step(1)
    for j in range(1, n_d):
        collect(j)
    combine()
    weight_ready()
    local[5].wait()
    ring_start()
    advance(2, 0, 1)
    attend_step(2)
    ring_step(1)
    advance(3, 0, 1)
    ring_step(2)
    attend_step(3)
    finish_self()
    local[6].wait()
    ring_end()
    for rb in range(ROW_BLOCKS):
        rs = slice(rb * rb_rows, (rb + 1) * rb_rows)
        z_copy(rb).wait_recv()
        mixed_ref[rs] = (mine[rs] + zrecv[rs].astype(jnp.float32)).astype(jnp.bfloat16)

    for m in range(1, n_d):
        id_copy(m).wait_send()
        query_copy(m).wait_send()
        weight_copy(m).wait_send()
        out_copy(m).wait_send()
        stat_copy(m).wait_send()
    for step in range(half):
        for part in (0, 1):
            if plus_has(step, part):
                pl.when(jnp.logical_and(y - step >= 0, y < n_y - 1))(
                    lambda step=step, part=part: plus_copy(step, part).wait_send())
            if minus_has(step, part):
                pl.when(minus_good((y + step) % n_y, part))(
                    lambda step=step, part=part: minus_copy(step, part).wait_send())
        wplus(step).wait_send()
        if step < half - 1:
            wminus(step).wait_send()
    for source in range(n_y):
        for part in (0, 1):
            pl.when(source < y)(lambda source=source, part=part: pass_copy(source, part, False).wait_send())
        wpass(source).wait_send()
    for part in (0, 1):
        pl.when(c == 0)(lambda part=part: pass_copy(y, part, True).wait_send())
    for side in (0, 1):
        for step in range(n_x - 1):
            for rb in range(ROW_BLOCKS):
                ring_copy(side, step, rb).wait_send()
    for rb in range(ROW_BLOCKS):
        z_copy(rb).wait_send()


def hand_over(a_ref, b_ref, a_out, b_out, sem):
    copies = [pltpu.make_async_copy(a_ref, a_out, sem.at[0]), pltpu.make_async_copy(b_ref, b_out, sem.at[1])]
    for copy in copies:
        copy.start()
    for copy in copies:
        copy.wait()


def shards(sizes, hidden_in, queries, keys, values, cross_queries, neighbours, database, out_weight):
    n_y, n_d, n_x = sizes
    half = n_y // 2
    rows, width = queries.shape[1:]
    heads = width // DH
    spans = rows // SPAN
    n_c = 2 * n_y
    piece = width // n_c
    cols = out_weight.shape[1]
    half_w = cols // 2
    bf16, f32 = jnp.bfloat16, jnp.float32
    vm, dma = pltpu.VMEM, pltpu.SemaphoreType.DMA
    any_spec = pl.BlockSpec(memory_space=pl.ANY)
    scratch = [vm((spans, SPAN, width), bf16) for _ in range(n_d)] + [
        vm((n_c, 2, rows, width), bf16),
        vm((rows, width), bf16),
        vm((rows, width), bf16),
        pltpu.SMEM((spans, NEIGH), jnp.int32),
        vm((n_d, 8, 128), jnp.int32),
        pltpu.SMEM((n_d, 8, 128), jnp.int32),
        vm(database.shape, bf16),
        vm((n_c, n_d, piece, cols), bf16),
        vm((max(n_d - 1, 1), SLOTS, SPAN, width), bf16),
        vm((n_d, SLOTS, SPAN, width), bf16),
        vm((n_d - 1, SPAN, 128), f32),
        vm((n_d, SPAN, 128), f32),
        vm((n_d, SLOTS, SPAN, 128), f32),
        vm((rows, width), bf16),
        vm((2 * (n_x - 1), rows, half_w), f32),
        vm((2, n_x - 1, rows, half_w), bf16),
        vm((2, n_x - 1, rows, half_w), bf16),
        vm((rows, half_w), f32),
        vm((rows, half_w), bf16),
        vm((rows, half_w), bf16),
        vm((heads, rows, 1), f32),
        vm((heads, rows, 1), f32),
        vm((heads, rows, DH), f32),
        dma((8,)),
        dma((half, 2)), dma((half, 2)), dma((half, 2)), dma((half, 2)),
        dma((n_y, 2)), dma((n_y, 2)),
        dma((n_d,)), dma((n_d,)), dma((n_d,)), dma((n_d,)), dma((n_d,)),
        dma((n_d,)), dma((n_d,)), dma((n_d,)), dma((n_d,)),
        dma((n_d,)), dma((n_d,)),
        dma((half,)), dma((half,)), dma((half,)), dma((half,)),
        dma((n_y,)), dma((n_y,)),
        dma((2, n_x - 1, ROW_BLOCKS)), dma((2, n_x - 1, ROW_BLOCKS)),
        dma((ROW_BLOCKS,)), dma((ROW_BLOCKS,)),
    ]
    attended, mixed = pl.pallas_call(
        functools.partial(layer, sizes),
        out_shape=(
            jax.ShapeDtypeStruct((rows, width), bf16),
            jax.ShapeDtypeStruct((rows, half_w), bf16),
        ),
        in_specs=[any_spec] * 8,
        out_specs=(pl.BlockSpec(memory_space=pltpu.VMEM), pl.BlockSpec(memory_space=pltpu.VMEM)),
        scratch_shapes=scratch,
        compiler_params=pltpu.CompilerParams(
            collective_id=0, has_side_effects=True, vmem_limit_bytes=56 * 1024 * 1024
        ),
        name="layer",
    )(
        neighbours,
        hidden_in[0],
        queries[0],
        keys[0],
        values[0],
        cross_queries[0].reshape(spans, SPAN, width),
        database,
        out_weight.reshape(n_c, piece, cols),
    )
    attended, mixed = pl.pallas_call(
        hand_over,
        out_shape=(
            jax.ShapeDtypeStruct((rows, width), bf16),
            jax.ShapeDtypeStruct((rows, half_w), bf16),
        ),
        in_specs=[pl.BlockSpec(memory_space=pltpu.VMEM)] * 2,
        out_specs=(any_spec, any_spec),
        scratch_shapes=[dma((2,))],
        name="hand_over",
    )(attended, mixed)
    return attended[None], mixed[None]


def solution(mesh):
    sizes = (mesh.shape["ctx"] // 2, mesh.shape["db"], mesh.shape["tp"] // 2)
    in_specs = (
        P("db", "ctx", "tp"),
        P("db", "ctx", "tp"),
        P("db", "ctx", "tp"),
        P("db", "ctx", "tp"),
        P("db", "ctx", "tp"),
        P("db", "ctx", None),
        P(None, "db", None, "tp"),
        P("tp", "db"),
    )
    out_specs = (P("db", "ctx", "tp"), P("db", "ctx", "tp"))
    return jax.shard_map(
        functools.partial(shards, sizes), mesh=mesh, in_specs=in_specs, out_specs=out_specs, check_vma=False
    )
```

```python
import functools
import math

import jax
import jax.numpy as jnp
from jax import lax
from jax.experimental import pallas as pl
from jax.experimental.pallas import tpu as pltpu
from jax.sharding import PartitionSpec as P

DH = 128
SPAN = 64
NEIGH = 2
SLOTS = 4
PER_SHARD = 8
ROW_BLOCKS = 2
CUTS = 1
MESH = pl.DeviceIdType.MESH
SCALE = 1.0 / math.sqrt(DH)
SCALE2 = SCALE * math.log2(math.e)
LOG2E = math.log2(math.e)
NT = (((1,), (1,)), ((), ()))


def remote(src, dst, send_sem, recv_sem, **where):
    return pltpu.make_async_remote_copy(
        src_ref=src, dst_ref=dst, send_sem=send_sem, recv_sem=recv_sem, device_id=where, device_id_type=MESH
    )


def layer(sizes, near_hbm, hid_hbm, q_hbm, k_hbm, v_hbm, cq_hbm, db_hbm, w_hbm, att_ref, mixed_ref, *scratch):
    n_y, n_d, n_x = sizes
    half = n_y // 2
    (kv, qv, hid, near_ref, nbv, nbs, dbv, wg, osend, orecv, stsend, strecv, stat, co, terms, xsend, xrecv,
     mine, zsend, zrecv, mref, lref, acc,
     loc_sem, ps, pr, ms, mr, cs, cr, qs, qr, ns, nr, nl, os_, or_, ss, sr, wzs, wzr, wps, wpr, wms, wmr, wcs, wcr,
     xs, xr, zs, zr) = scratch[n_d:]
    cqa = scratch[:n_d]
    rows = qv.shape[0]
    width = qv.shape[1]
    heads = width // DH
    spans = rows // SPAN
    entries = spans * NEIGH

    i = lax.axis_index("ctx")
    d = lax.axis_index("db")
    t = lax.axis_index("tp")
    y, c = i // 2, i % 2
    x, zh = t // 2, t % 2
    other = i + 1 - 2 * c
    up = (i + 2) % (2 * n_y)
    down = (i + 2 * n_y - 2) % (2 * n_y)
    right = ((x + 1) % n_x) * 2 + zh
    left = ((x + n_x - 1) % n_x) * 2 + zh
    across = x * 2 + 1 - zh

    loads = [
        (q_hbm, qv), (k_hbm, kv.at[i, 0]), (v_hbm, kv.at[i, 1]), (cq_hbm, cqa[0]),
        (db_hbm, dbv), (w_hbm, wg.at[:, 0]), (hid_hbm, hid), (near_hbm.at[0], near_ref),
    ]
    local = [pltpu.make_async_copy(a, b, loc_sem.at[n]) for n, (a, b) in enumerate(loads)]
    for n in (7, 3, 4, 0, 1, 2, 5, 6):
        local[n].start()
    barrier = pltpu.get_barrier_semaphore()
    greet = [dict(ctx=up), dict(ctx=down), dict(ctx=other), dict(tp=right), dict(tp=left), dict(tp=across)]
    greet += [dict(db=(d + m) % n_d) for m in range(1, n_d)]
    for where in greet:
        pl.semaphore_signal(barrier, inc=1, device_id=where, device_id_type=MESH)

    local[7].wait()
    lane = lax.broadcasted_iota(jnp.int32, (8, 128), 1)
    ids = jnp.zeros((8, 128), jnp.int32)
    for n in range(entries):
        ids = jnp.where(lane == n, near_ref[n // NEIGH, n % NEIGH], ids)
    nbv[0] = ids
    pl.semaphore_wait(barrier, len(greet))

    def id_copy(m):
        return remote(nbv.at[0], nbv.at[n_d - m], ns.at[n_d - m], nr.at[n_d - m], db=(d + m) % n_d)

    def query_copy(m):
        return remote(cq_hbm, cqa[n_d - m], qs.at[n_d - m], qr.at[n_d - m], db=(d + m) % n_d)

    def weight_copy(m):
        j = n_d - m
        return remote(w_hbm.at[i], wg.at[i, j], wzs.at[j], wzr.at[j], db=(d + m) % n_d)

    def plus_has(step, part):
        return step < half - 1 or part == 0

    def plus_copy(step, part):
        slot = 2 * (y - step) + c
        src = (k_hbm, v_hbm)[part] if step == 0 else kv.at[slot, part]
        return remote(src, kv.at[slot, part], ps.at[step, part], pr.at[step, part], ctx=up)

    def minus_has(step, part):
        return part == 1 or step <= half - 2

    def minus_good(source, part):
        return source <= (half - 1 if part == 1 else half - 2)

    def minus_copy(step, part):
        slot = 2 * ((y + step) % n_y) + c
        src = (k_hbm, v_hbm)[part] if step == 0 else kv.at[slot, part]
        return remote(src, kv.at[slot, part], ms.at[step, part], mr.at[step, part], ctx=down)

    def pass_copy(source, part, own):
        slot = 2 * source + c
        src = (k_hbm, v_hbm)[part] if own else kv.at[slot, part]
        return remote(src, kv.at[slot, part], cs.at[source, part], cr.at[source, part], ctx=other)

    def kv_start(part):
        pl.when(y < n_y - 1)(lambda: plus_copy(0, part).start())
        pl.when(minus_good(y, part))(lambda: minus_copy(0, part).start())
        pl.when(c == 0)(lambda: pass_copy(y, part, True).start())

    for m in range(1, n_d):
        id_copy(m).start()
    for m in range(1, n_d):
        weight_copy(m).start()
    for m in range(1, n_d):
        query_copy(m).start()
    kv_start(0)

    def head(h):
        return slice(h * DH, (h + 1) * DH)

    def attend_first():
        row = lax.broadcasted_iota(jnp.int32, (rows, rows), 0)
        col = lax.broadcasted_iota(jnp.int32, (rows, rows), 1)
        keep = col <= row
        scores = [
            lax.dot_general(qv[:, head(h)], kv[i, 0, :, head(h)], NT, preferred_element_type=jnp.float32)
            for h in range(heads)
        ]
        weights = []
        for h in range(heads):
            s = jnp.where(keep, scores[h], -1e30)
            peak = jnp.max(s, axis=-1, keepdims=True)
            p = jnp.exp2((s - peak) * SCALE2)
            mref[h] = peak
            lref[h] = jnp.sum(p, axis=-1, keepdims=True)
            weights.append(p.astype(jnp.bfloat16))
        for h in range(heads):
            acc[h] = jnp.dot(weights[h], kv[i, 1, :, head(h)], preferred_element_type=jnp.float32)

    def attend(start, count):
        for h in range(heads):
            keys = kv[pl.ds(start, count), 0, :, head(h)].reshape(count * rows, DH)
            vals = kv[pl.ds(start, count), 1, :, head(h)].reshape(count * rows, DH)
            for part in range(CUTS):
                rs = slice(part * rows // CUTS, (part + 1) * rows // CUTS)
                s = lax.dot_general(qv[rs, head(h)], keys, NT, preferred_element_type=jnp.float32)
                before = mref[h, rs]
                peak = jnp.maximum(before, jnp.max(s, axis=-1, keepdims=True))
                p = jnp.exp2((s - peak) * SCALE2)
                factor = jnp.exp2((before - peak) * SCALE2)
                mref[h, rs] = peak
                lref[h, rs] = lref[h, rs] * factor + jnp.sum(p, axis=-1, keepdims=True)
                fresh = jnp.dot(p.astype(jnp.bfloat16), vals, preferred_element_type=jnp.float32)
                acc[h, rs] = acc[h, rs] * factor + fresh

    def wait_passed(source):
        for part in (0, 1):
            slot = 2 * source + 1 - c
            remote(
                kv.at[slot, part], kv.at[slot, part], cs.at[source, part], cr.at[source, part], ctx=other
            ).wait_recv()

    def attend_pair(source):
        wait_passed(source)
        attend(2 * source, 2)

    def advance(step, *parts):
        for part in parts:
            if plus_has(step, part):
                source = y - 1 - step

                @pl.when(source >= 0)
                def _():
                    slot = 2 * source + c
                    remote(
                        kv.at[slot, part], kv.at[slot, part], ps.at[step, part], pr.at[step, part], ctx=up
                    ).wait_recv()
                    if step + 1 < half and plus_has(step + 1, part):
                        pl.when(y < n_y - 1)(lambda: plus_copy(step + 1, part).start())
                    pass_copy(source, part, False).start()

            if minus_has(step, part):
                source2 = (y + 1 + step) % n_y

                @pl.when(minus_good(source2, part))
                def _():
                    slot = 2 * source2 + c
                    remote(
                        kv.at[slot, part], kv.at[slot, part], ms.at[step, part], mr.at[step, part], ctx=down
                    ).wait_recv()
                    if step + 1 < half and minus_has(step + 1, part):
                        minus_copy(step + 1, part).start()
                    pl.when(source2 < y)(lambda: pass_copy(source2, part, False).start())

    def attend_step(step):
        if step < half - 1:
            pl.when(y - 1 - step >= 0)(lambda: attend_pair(y - 1 - step))
            pl.when(y + 1 + step >= n_y)(lambda: attend_pair(y + 1 + step - n_y))
        else:
            pl.when(y >= half)(lambda: attend_pair(y - half))

    def wplus(step):
        slot = 2 * ((y - step + n_y) % n_y) + c
        piece = wg.at[slot, pl.ds(1, n_d - 1)]
        return remote(piece, piece, wps.at[step], wpr.at[step], ctx=up)

    def wminus(step):
        slot = 2 * ((y + step) % n_y) + c
        piece = wg.at[slot, pl.ds(1, n_d - 1)]
        return remote(piece, piece, wms.at[step], wmr.at[step], ctx=down)

    def wpass(source):
        piece = wg.at[2 * source + c, pl.ds(1, n_d - 1)]
        return remote(piece, piece, wcs.at[source], wcr.at[source], ctx=other)

    def weight_step(step):
        if step == 0:
            for j in range(1, n_d):
                remote(w_hbm.at[i], wg.at[i, j], wzs.at[j], wzr.at[j], db=d).wait_recv()
            source = y
        else:
            source = (y - step + n_y) % n_y
            piece = wg.at[2 * source + c, pl.ds(1, n_d - 1)]
            remote(piece, piece, wps.at[step - 1], wpr.at[step - 1], ctx=up).wait_recv()
        if step < half:
            wplus(step).start()
        wpass(source).start()
        if step < half - 1 and step == 0:
            wminus(0).start()
        if 1 <= step <= half - 1:
            source2 = (y + step) % n_y
            piece2 = wg.at[2 * source2 + c, pl.ds(1, n_d - 1)]
            remote(piece2, piece2, wms.at[step - 1], wmr.at[step - 1], ctx=down).wait_recv()
            if step < half - 1:
                wminus(step).start()
            wpass(source2).start()

    def weight_ready():
        for source in range(n_y):
            piece = wg.at[2 * source + 1 - c, pl.ds(1, n_d - 1)]
            remote(piece, piece, wcs.at[source], wcr.at[source], ctx=other).wait_recv()

    def id_move(j):
        return pltpu.make_async_copy(nbv.at[j], nbs.at[j], nl.at[j])

    def block_id(j, n):
        return near_ref[n // NEIGH, n % NEIGH] if j == 0 else nbs[j, 0, n]

    def lookups(j):
        spots = [jnp.int32(0)] * SLOTS
        blocks = [jnp.int32(0)] * SLOTS
        seen = jnp.int32(0)
        for n in range(entries):
            block = block_id(j, n)
            hit = (block // PER_SHARD) == d
            for k in range(min(n + 1, SLOTS)):
                take = jnp.logical_and(hit, seen == k)
                spots[k] = jnp.where(take, n // NEIGH, spots[k])
                blocks[k] = jnp.where(take, block % PER_SHARD, blocks[k])
            seen = seen + jnp.where(hit, 1, 0)
        return spots, blocks

    def serve(j, found):
        spots, blocks = found
        if j > 0:
            remote(cq_hbm, cqa[j], qs.at[j], qr.at[j], db=d).wait_recv()
        lanes = lax.broadcasted_iota(jnp.int32, (SPAN, 128), 1)
        st = jnp.zeros((SPAN, 128), jnp.float32)
        out = orecv.at[0] if j == 0 else osend.at[j - 1]
        zero = jnp.zeros((SPAN, DH), jnp.bfloat16)
        scores, vals = [], []
        for k in range(SLOTS):
            query = cqa[j][spots[k]]
            keys = dbv[0, blocks[k]]
            vals.append(dbv[1, blocks[k]])
            for g in range(heads // 2):
                first = query[:, 2 * g * DH:(2 * g + 1) * DH]
                second = query[:, (2 * g + 1) * DH:(2 * g + 2) * DH]
                both = jnp.concatenate(
                    [jnp.concatenate([first, zero], axis=1), jnp.concatenate([zero, second], axis=1)], axis=0
                )
                scores.append(
                    lax.dot_general(
                        both, keys[:, 2 * g * DH:(2 * g + 2) * DH], NT, preferred_element_type=jnp.float32
                    )
                )
        s = jnp.concatenate(scores, axis=0)
        peak = jnp.max(s, axis=-1, keepdims=True)
        p = jnp.exp2((s - peak) * SCALE2)
        total = jnp.sum(p, axis=-1, keepdims=True)
        inv = 1.0 / total
        level = peak * SCALE2 + jnp.log(total) * LOG2E
        p = p.astype(jnp.bfloat16)
        for k in range(SLOTS):
            for g in range(heads // 2):
                n = k * heads + 2 * g
                o = jnp.dot(
                    p[n * SPAN:(n + 2) * SPAN], vals[k][:, 2 * g * DH:(2 * g + 2) * DH],
                    preferred_element_type=jnp.float32,
                )
                for e in (0, 1):
                    rs = slice((n + e) * SPAN, (n + e + 1) * SPAN)
                    part = o[e * SPAN:(e + 1) * SPAN, e * DH:(e + 1) * DH] * inv[rs]
                    out[k, :, (2 * g + e) * DH:(2 * g + e + 1) * DH] = part.astype(jnp.bfloat16)
                    st = jnp.where(lanes == n + e, level[rs], st)
        if j == 0:
            strecv[0] = st
        else:
            stsend[j - 1] = st
            out_copy(j).start()
            stat_copy(j).start()

    def out_copy(j):
        return remote(osend.at[j - 1], orecv.at[n_d - j], os_.at[n_d - j], or_.at[n_d - j], db=(d + j) % n_d)

    def stat_copy(j):
        return remote(stsend.at[j - 1], strecv.at[n_d - j], ss.at[n_d - j], sr.at[n_d - j], db=(d + j) % n_d)

    def collect(j):
        if j > 0:
            remote(osend.at[0], orecv.at[j], os_.at[j], or_.at[j], db=d).wait_recv()
            remote(stsend.at[0], strecv.at[j], ss.at[j], sr.at[j], db=d).wait_recv()
        packed = strecv[j]
        stat[j, 0] = packed
        for k in range(1, SLOTS):
            stat[j, k] = pltpu.roll(packed, 128 - k * heads, 1)

    def combine():
        places = []
        owners = []
        for n in range(entries):
            owner = block_id(0, n) // PER_SHARD
            rank = jnp.int32(0)
            for earlier in owners:
                rank = rank + jnp.where(earlier == owner, 1, 0)
            owners.append(owner)
            places.append(((owner - d + n_d) % n_d, jnp.minimum(rank, SLOTS - 1)))
        for u in range(spans):
            (oa, ka), (ob, kb) = places[2 * u], places[2 * u + 1]
            sa, sb = stat[oa, ka], stat[ob, kb]
            peak = jnp.maximum(sa, sb)
            ea = jnp.exp2(sa - peak)
            eb = jnp.exp2(sb - peak)
            inv = 1.0 / (ea + eb)
            ea, eb = ea * inv, eb * inv
            va, vb = orecv[oa, ka], orecv[ob, kb]
            for h in range(heads):
                hs = slice(h * DH, (h + 1) * DH)
                o = va[:, hs].astype(jnp.float32) * ea[:, h:h + 1] + vb[:, hs].astype(jnp.float32) * eb[:, h:h + 1]
                co[u * SPAN:(u + 1) * SPAN, hs] = o.astype(jnp.bfloat16)

    half_w = terms.shape[2]

    def project(rho, side):
        j = ((x + rho) % n_x - d + n_d) % n_d
        block = wg[:, j, :, side * half_w:(side + 1) * half_w].reshape(width, half_w)
        return jnp.dot(co[...], block, preferred_element_type=jnp.float32)

    rb_rows = rows // ROW_BLOCKS

    def ring_copy(side, step, rb):
        rs = pl.ds(rb * rb_rows, rb_rows)
        return remote(
            xsend.at[side, step, rs], xrecv.at[side, step, rs], xs.at[side, step, rb], xr.at[side, step, rb],
            tp=(right, left)[side],
        )

    def rho_of(side, step):
        return (n_x - 1 - step) % n_x if side == 0 else (1 + step) % n_x

    def ring_start():
        for side in (0, 1):
            xsend[side, 0] = project(rho_of(side, 0), side).astype(jnp.bfloat16)
            for rb in range(ROW_BLOCKS):
                ring_copy(side, 0, rb).start()
        for step in range(1, n_x):
            for side in (0, 1):
                terms[side * (n_x - 1) + step - 1] = project(rho_of(side, step), side)

    def ring_step(step):
        for rb in range(ROW_BLOCKS):
            rs = slice(rb * rb_rows, (rb + 1) * rb_rows)
            for side in (0, 1):
                ring_copy(side, step - 1, rb).wait_recv()
                total = xrecv[side, step - 1, rs].astype(jnp.float32) + terms[side * (n_x - 1) + step - 1, rs]
                xsend[side, step, rs] = total.astype(jnp.bfloat16)
                ring_copy(side, step, rb).start()

    def z_copy(rb):
        rs = pl.ds(rb * rb_rows, rb_rows)
        return remote(zsend.at[rs], zrecv.at[rs], zs.at[rb], zr.at[rb], tp=across)

    def ring_end():
        for rb in range(ROW_BLOCKS):
            rs = slice(rb * rb_rows, (rb + 1) * rb_rows)
            sums = []
            for side in (0, 1):
                ring_copy(side, n_x - 2, rb).wait_recv()
                sums.append(
                    xrecv[side, n_x - 2, rs].astype(jnp.float32) + terms[side * (n_x - 1) + n_x - 2, rs]
                )
            zsend[rs] = jnp.where(zh == 0, sums[1], sums[0]).astype(jnp.bfloat16)
            z_copy(rb).start()
            mine[rs] = jnp.where(zh == 0, sums[0], sums[1]) + hid[rs].astype(jnp.float32)

    def finish_self():
        for h in range(heads):
            hs = slice(h * DH, (h + 1) * DH)
            att_ref[:, hs] = (acc[h] / lref[h]).astype(jnp.bfloat16)

    for n in (3, 4):
        local[n].wait()
    serve(0, lookups(0))
    for n in (0, 1, 2):
        local[n].wait()
    attend_first()
    for j in range(1, n_d):
        remote(nbv.at[0], nbv.at[j], ns.at[j], nr.at[j], db=d).wait_recv()
        id_move(j).start()
    weight_step(0)
    kv_start(1)
    found = {}
    for j in range(1, n_d):
        id_move(j).wait()
        found[j] = lookups(j)
    collect(0)
    weight_step(1)
    serve(1, found[1])
    weight_step(2)
    advance(0, 0)
    serve(3, found[3])
    weight_step(3)
    serve(2, found[2])
    weight_step(4)
    advance(0, 1)
    pl.when(c == 1)(lambda: wait_passed(y))
    pl.when(c == 1)(lambda: attend(i - 1, 1))
    attend_step(0)
    advance(1, 0, 1)
    attend_step(1)
    for j in range(1, n_d):
        collect(j)
    combine()
    weight_ready()
    local[5].wait()
    ring_start()
    advance(2, 0, 1)
    attend_step(2)
    ring_step(1)
    advance(3, 0, 1)
    ring_step(2)
    attend_step(3)
    finish_self()
    local[6].wait()
    ring_end()
    for rb in range(ROW_BLOCKS):
        rs = slice(rb * rb_rows, (rb + 1) * rb_rows)
        z_copy(rb).wait_recv()
        mixed_ref[rs] = (mine[rs] + zrecv[rs].astype(jnp.float32)).astype(jnp.bfloat16)

    for m in range(1, n_d):
        id_copy(m).wait_send()
        query_copy(m).wait_send()
        weight_copy(m).wait_send()
        out_copy(m).wait_send()
        stat_copy(m).wait_send()
    for step in range(half):
        for part in (0, 1):
            if plus_has(step, part):
                pl.when(jnp.logical_and(y - step >= 0, y < n_y - 1))(
                    lambda step=step, part=part: plus_copy(step, part).wait_send())
            if minus_has(step, part):
                pl.when(minus_good((y + step) % n_y, part))(
                    lambda step=step, part=part: minus_copy(step, part).wait_send())
        wplus(step).wait_send()
        if step < half - 1:
            wminus(step).wait_send()
    for source in range(n_y):
        for part in (0, 1):
            pl.when(source < y)(lambda source=source, part=part: pass_copy(source, part, False).wait_send())
        wpass(source).wait_send()
    for part in (0, 1):
        pl.when(c == 0)(lambda part=part: pass_copy(y, part, True).wait_send())
    for side in (0, 1):
        for step in range(n_x - 1):
            for rb in range(ROW_BLOCKS):
                ring_copy(side, step, rb).wait_send()
    for rb in range(ROW_BLOCKS):
        z_copy(rb).wait_send()


def hand_over(a_ref, b_ref, a_out, b_out, sem):
    copies = [pltpu.make_async_copy(a_ref, a_out, sem.at[0]), pltpu.make_async_copy(b_ref, b_out, sem.at[1])]
    for copy in copies:
        copy.start()
    for copy in copies:
        copy.wait()


def shards(sizes, hidden_in, queries, keys, values, cross_queries, neighbours, database, out_weight):
    n_y, n_d, n_x = sizes
    half = n_y // 2
    rows, width = queries.shape[1:]
    heads = width // DH
    spans = rows // SPAN
    n_c = 2 * n_y
    piece = width // n_c
    cols = out_weight.shape[1]
    half_w = cols // 2
    bf16, f32 = jnp.bfloat16, jnp.float32
    vm, dma = pltpu.VMEM, pltpu.SemaphoreType.DMA
    any_spec = pl.BlockSpec(memory_space=pl.ANY)
    scratch = [vm((spans, SPAN, width), bf16) for _ in range(n_d)] + [
        vm((n_c, 2, rows, width), bf16),
        vm((rows, width), bf16),
        vm((rows, width), bf16),
        pltpu.SMEM((spans, NEIGH), jnp.int32),
        vm((n_d, 8, 128), jnp.int32),
        pltpu.SMEM((n_d, 8, 128), jnp.int32),
        vm(database.shape, bf16),
        vm((n_c, n_d, piece, cols), bf16),
        vm((max(n_d - 1, 1), SLOTS, SPAN, width), bf16),
        vm((n_d, SLOTS, SPAN, width), bf16),
        vm((n_d - 1, SPAN, 128), f32),
        vm((n_d, SPAN, 128), f32),
        vm((n_d, SLOTS, SPAN, 128), f32),
        vm((rows, width), bf16),
        vm((2 * (n_x - 1), rows, half_w), f32),
        vm((2, n_x - 1, rows, half_w), bf16),
        vm((2, n_x - 1, rows, half_w), bf16),
        vm((rows, half_w), f32),
        vm((rows, half_w), bf16),
        vm((rows, half_w), bf16),
        vm((heads, rows, 1), f32),
        vm((heads, rows, 1), f32),
        vm((heads, rows, DH), f32),
        dma((8,)),
        dma((half, 2)), dma((half, 2)), dma((half, 2)), dma((half, 2)),
        dma((n_y, 2)), dma((n_y, 2)),
        dma((n_d,)), dma((n_d,)), dma((n_d,)), dma((n_d,)), dma((n_d,)),
        dma((n_d,)), dma((n_d,)), dma((n_d,)), dma((n_d,)),
        dma((n_d,)), dma((n_d,)),
        dma((half,)), dma((half,)), dma((half,)), dma((half,)),
        dma((n_y,)), dma((n_y,)),
        dma((2, n_x - 1, ROW_BLOCKS)), dma((2, n_x - 1, ROW_BLOCKS)),
        dma((ROW_BLOCKS,)), dma((ROW_BLOCKS,)),
    ]
    attended, mixed = pl.pallas_call(
        functools.partial(layer, sizes),
        out_shape=(
            jax.ShapeDtypeStruct((rows, width), bf16),
            jax.ShapeDtypeStruct((rows, half_w), bf16),
        ),
        in_specs=[any_spec] * 8,
        out_specs=(pl.BlockSpec(memory_space=pltpu.VMEM), pl.BlockSpec(memory_space=pltpu.VMEM)),
        scratch_shapes=scratch,
        compiler_params=pltpu.CompilerParams(
            collective_id=0, has_side_effects=True, vmem_limit_bytes=56 * 1024 * 1024
        ),
        name="layer",
    )(
        neighbours,
        hidden_in[0],
        queries[0],
        keys[0],
        values[0],
        cross_queries[0].reshape(spans, SPAN, width),
        database,
        out_weight.reshape(n_c, piece, cols),
    )
    attended, mixed = pl.pallas_call(
        hand_over,
        out_shape=(
            jax.ShapeDtypeStruct((rows, width), bf16),
            jax.ShapeDtypeStruct((rows, half_w), bf16),
        ),
        in_specs=[pl.BlockSpec(memory_space=pltpu.VMEM)] * 2,
        out_specs=(any_spec, any_spec),
        scratch_shapes=[dma((2,))],
        name="hand_over",
    )(attended, mixed)
    return attended[None], mixed[None]


def solution(mesh):
    sizes = (mesh.shape["ctx"] // 2, mesh.shape["db"], mesh.shape["tp"] // 2)
    in_specs = (
        P("db", "ctx", "tp"),
        P("db", "ctx", "tp"),
        P("db", "ctx", "tp"),
        P("db", "ctx", "tp"),
        P("db", "ctx", "tp"),
        P("db", "ctx", None),
        P(None, "db", None, "tp"),
        P("tp", "db"),
    )
    out_specs = (P("db", "ctx", "tp"), P("db", "ctx", "tp"))
    return jax.shard_map(
        functools.partial(shards, sizes), mesh=mesh, in_specs=in_specs, out_specs=out_specs, check_vma=False
    )
```

```python
import functools
import math

import jax
import jax.numpy as jnp
from jax import lax
from jax.experimental import pallas as pl
from jax.experimental.pallas import tpu as pltpu
from jax.sharding import PartitionSpec as P

DH = 128
SPAN = 64
NEIGH = 2
SLOTS = 4
PER_SHARD = 8
ROW_BLOCKS = 2
CUTS = 1
MESH = pl.DeviceIdType.MESH
SCALE = 1.0 / math.sqrt(DH)
SCALE2 = SCALE * math.log2(math.e)
LOG2E = math.log2(math.e)
NT = (((1,), (1,)), ((), ()))


def remote(src, dst, send_sem, recv_sem, **where):
    return pltpu.make_async_remote_copy(
        src_ref=src, dst_ref=dst, send_sem=send_sem, recv_sem=recv_sem, device_id=where, device_id_type=MESH
    )


def layer(sizes, near_hbm, hid_hbm, q_hbm, k_hbm, v_hbm, cq_hbm, db_hbm, w_hbm, att_ref, mixed_ref, *scratch):
    n_y, n_d, n_x = sizes
    half = n_y // 2
    (kv, qv, hid, near_ref, nbv, nbs, dbv, wg, osend, orecv, stsend, strecv, stat, co, terms, xsend, xrecv,
     mine, zsend, zrecv, mref, lref, acc,
     loc_sem, ps, pr, ms, mr, cs, cr, qs, qr, ns, nr, nl, os_, or_, ss, sr, wzs, wzr, wps, wpr, wms, wmr, wcs, wcr,
     xs, xr, zs, zr) = scratch[2 * n_d - 1:]
    hops = n_d - 1
    own_q, cq_near = scratch[0], (scratch[1:n_d], scratch[n_d:2 * n_d - 1])
    rows = qv.shape[0]
    width = qv.shape[1]
    heads = width // DH
    spans = rows // SPAN
    entries = spans * NEIGH

    i = lax.axis_index("ctx")
    d = lax.axis_index("db")
    t = lax.axis_index("tp")
    y, c = i // 2, i % 2
    x, zh = t // 2, t % 2
    other = i + 1 - 2 * c
    up = (i + 2) % (2 * n_y)
    down = (i + 2 * n_y - 2) % (2 * n_y)
    right = ((x + 1) % n_x) * 2 + zh
    left = ((x + n_x - 1) % n_x) * 2 + zh
    across = x * 2 + 1 - zh

    loads = [
        (q_hbm, qv), (k_hbm, kv.at[i, 0]), (v_hbm, kv.at[i, 1]), (cq_hbm, own_q),
        (db_hbm, dbv), (w_hbm, wg.at[:, 0]), (hid_hbm, hid), (near_hbm.at[0], near_ref),
    ]
    local = [pltpu.make_async_copy(a, b, loc_sem.at[n]) for n, (a, b) in enumerate(loads)]
    for n in (7, 3, 4, 0, 1, 2, 5, 6):
        local[n].start()
    barrier = pltpu.get_barrier_semaphore()
    greet = [dict(ctx=up), dict(ctx=down), dict(ctx=other), dict(tp=right), dict(tp=left), dict(tp=across)]
    greet += [dict(db=(d + m) % n_d) for m in range(1, n_d)]
    for where in greet:
        pl.semaphore_signal(barrier, inc=1, device_id=where, device_id_type=MESH)

    local[7].wait()
    lane = lax.broadcasted_iota(jnp.int32, (8, 128), 1)
    ids = jnp.zeros((8, 128), jnp.int32)
    for n in range(entries):
        ids = jnp.where(lane == n, near_ref[n // NEIGH, n % NEIGH], ids)
    nbv[0] = ids
    pl.semaphore_wait(barrier, len(greet))

    def id_copy(m):
        return remote(nbv.at[0], nbv.at[n_d - m], ns.at[n_d - m], nr.at[n_d - m], db=(d + m) % n_d)

    def there(side, hop):
        return d - 1 - hop >= 0 if side == 0 else d + 1 + hop < n_d

    def asker(side, hop):
        return d - 1 - hop if side == 0 else d + 1 + hop

    def query_copy(side, hop):
        src = cq_hbm if hop == 0 else cq_near[side][hop - 1]
        return remote(
            src, cq_near[side][hop], qs.at[side, hop], qr.at[side, hop], db=d + 1 - 2 * side
        )

    def query_goes(side, hop):
        if side == 0:
            return jnp.logical_and(d - hop >= 0, d < n_d - 1)
        return jnp.logical_and(d + hop < n_d, d > 0)

    def query_step(hop):
        for side in (0, 1):

            @pl.when(there(side, hop))
            def _():
                remote(cq_hbm, cq_near[side][hop], qs.at[side, hop], qr.at[side, hop], db=d).wait_recv()
                if hop + 1 < hops:
                    pl.when(query_goes(side, hop + 1))(lambda: query_copy(side, hop + 1).start())

    def weight_copy(m):
        j = n_d - m
        return remote(w_hbm.at[i], wg.at[i, j], wzs.at[j], wzr.at[j], db=(d + m) % n_d)

    def plus_has(step, part):
        return step < half - 1 or part == 0

    def plus_copy(step, part):
        slot = 2 * (y - step) + c
        src = (k_hbm, v_hbm)[part] if step == 0 else kv.at[slot, part]
        return remote(src, kv.at[slot, part], ps.at[step, part], pr.at[step, part], ctx=up)

    def minus_has(step, part):
        return part == 1 or step <= half - 2

    def minus_good(source, part):
        return source <= (half - 1 if part == 1 else half - 2)

    def minus_copy(step, part):
        slot = 2 * ((y + step) % n_y) + c
        src = (k_hbm, v_hbm)[part] if step == 0 else kv.at[slot, part]
        return remote(src, kv.at[slot, part], ms.at[step, part], mr.at[step, part], ctx=down)

    def pass_copy(source, part, own):
        slot = 2 * source + c
        src = (k_hbm, v_hbm)[part] if own else kv.at[slot, part]
        return remote(src, kv.at[slot, part], cs.at[source, part], cr.at[source, part], ctx=other)

    def kv_start(part):
        pl.when(y < n_y - 1)(lambda: plus_copy(0, part).start())
        pl.when(minus_good(y, part))(lambda: minus_copy(0, part).start())
        pl.when(c == 0)(lambda: pass_copy(y, part, True).start())

    for m in range(1, n_d):
        id_copy(m).start()
    for m in range(1, n_d):
        weight_copy(m).start()
    for side in (0, 1):
        pl.when(query_goes(side, 0))(lambda side=side: query_copy(side, 0).start())
    kv_start(0)
    kv_start(1)

    def head(h):
        return slice(h * DH, (h + 1) * DH)

    def attend_first():
        row = lax.broadcasted_iota(jnp.int32, (rows, rows), 0)
        col = lax.broadcasted_iota(jnp.int32, (rows, rows), 1)
        keep = col <= row
        scores = [
            lax.dot_general(qv[:, head(h)], kv[i, 0, :, head(h)], NT, preferred_element_type=jnp.float32)
            for h in range(heads)
        ]
        weights = []
        for h in range(heads):
            s = jnp.where(keep, scores[h], -1e30)
            peak = jnp.max(s, axis=-1, keepdims=True)
            p = jnp.exp2((s - peak) * SCALE2)
            mref[h] = peak
            lref[h] = jnp.sum(p, axis=-1, keepdims=True)
            weights.append(p.astype(jnp.bfloat16))
        for h in range(heads):
            acc[h] = jnp.dot(weights[h], kv[i, 1, :, head(h)], preferred_element_type=jnp.float32)

    def attend(start, count):
        for h in range(heads):
            keys = kv[pl.ds(start, count), 0, :, head(h)].reshape(count * rows, DH)
            vals = kv[pl.ds(start, count), 1, :, head(h)].reshape(count * rows, DH)
            for part in range(CUTS):
                rs = slice(part * rows // CUTS, (part + 1) * rows // CUTS)
                s = lax.dot_general(qv[rs, head(h)], keys, NT, preferred_element_type=jnp.float32)
                before = mref[h, rs]
                peak = jnp.maximum(before, jnp.max(s, axis=-1, keepdims=True))
                p = jnp.exp2((s - peak) * SCALE2)
                factor = jnp.exp2((before - peak) * SCALE2)
                mref[h, rs] = peak
                lref[h, rs] = lref[h, rs] * factor + jnp.sum(p, axis=-1, keepdims=True)
                fresh = jnp.dot(p.astype(jnp.bfloat16), vals, preferred_element_type=jnp.float32)
                acc[h, rs] = acc[h, rs] * factor + fresh

    def wait_passed(source):
        for part in (0, 1):
            slot = 2 * source + 1 - c
            remote(
                kv.at[slot, part], kv.at[slot, part], cs.at[source, part], cr.at[source, part], ctx=other
            ).wait_recv()

    def attend_pair(source):
        wait_passed(source)
        attend(2 * source, 2)

    def advance(step, *parts):
        for part in parts:
            if plus_has(step, part):
                source = y - 1 - step

                @pl.when(source >= 0)
                def _():
                    slot = 2 * source + c
                    remote(
                        kv.at[slot, part], kv.at[slot, part], ps.at[step, part], pr.at[step, part], ctx=up
                    ).wait_recv()
                    if step + 1 < half and plus_has(step + 1, part):
                        pl.when(y < n_y - 1)(lambda: plus_copy(step + 1, part).start())
                    pass_copy(source, part, False).start()

            if minus_has(step, part):
                source2 = (y + 1 + step) % n_y

                @pl.when(minus_good(source2, part))
                def _():
                    slot = 2 * source2 + c
                    remote(
                        kv.at[slot, part], kv.at[slot, part], ms.at[step, part], mr.at[step, part], ctx=down
                    ).wait_recv()
                    if step + 1 < half and minus_has(step + 1, part):
                        minus_copy(step + 1, part).start()
                    pl.when(source2 < y)(lambda: pass_copy(source2, part, False).start())

    def attend_step(step):
        if step < half - 1:
            pl.when(y - 1 - step >= 0)(lambda: attend_pair(y - 1 - step))
            pl.when(y + 1 + step >= n_y)(lambda: attend_pair(y + 1 + step - n_y))
        else:
            pl.when(y >= half)(lambda: attend_pair(y - half))

    def wplus(step):
        slot = 2 * ((y - step + n_y) % n_y) + c
        piece = wg.at[slot, pl.ds(1, n_d - 1)]
        return remote(piece, piece, wps.at[step], wpr.at[step], ctx=up)

    def wminus(step):
        slot = 2 * ((y + step) % n_y) + c
        piece = wg.at[slot, pl.ds(1, n_d - 1)]
        return remote(piece, piece, wms.at[step], wmr.at[step], ctx=down)

    def wpass(source):
        piece = wg.at[2 * source + c, pl.ds(1, n_d - 1)]
        return remote(piece, piece, wcs.at[source], wcr.at[source], ctx=other)

    def weight_step(step):
        if step == 0:
            for j in range(1, n_d):
                remote(w_hbm.at[i], wg.at[i, j], wzs.at[j], wzr.at[j], db=d).wait_recv()
            source = y
        else:
            source = (y - step + n_y) % n_y
            piece = wg.at[2 * source + c, pl.ds(1, n_d - 1)]
            remote(piece, piece, wps.at[step - 1], wpr.at[step - 1], ctx=up).wait_recv()
        if step < half:
            wplus(step).start()
        wpass(source).start()
        if step < half - 1 and step == 0:
            wminus(0).start()
        if 1 <= step <= half - 1:
            source2 = (y + step) % n_y
            piece2 = wg.at[2 * source2 + c, pl.ds(1, n_d - 1)]
            remote(piece2, piece2, wms.at[step - 1], wmr.at[step - 1], ctx=down).wait_recv()
            if step < half - 1:
                wminus(step).start()
            wpass(source2).start()

    def weight_ready():
        for source in range(n_y):
            piece = wg.at[2 * source + 1 - c, pl.ds(1, n_d - 1)]
            remote(piece, piece, wcs.at[source], wcr.at[source], ctx=other).wait_recv()

    def id_move(j):
        return pltpu.make_async_copy(nbv.at[j], nbs.at[j], nl.at[j])

    def lookups(block_id):
        spots = [jnp.int32(0)] * SLOTS
        blocks = [jnp.int32(0)] * SLOTS
        seen = jnp.int32(0)
        for n in range(entries):
            block = block_id(n)
            hit = (block // PER_SHARD) == d
            for k in range(min(n + 1, SLOTS)):
                take = jnp.logical_and(hit, seen == k)
                spots[k] = jnp.where(take, n // NEIGH, spots[k])
                blocks[k] = jnp.where(take, block % PER_SHARD, blocks[k])
            seen = seen + jnp.where(hit, 1, 0)
        return spots, blocks

    def own_id(n):
        return near_ref[n // NEIGH, n % NEIGH]

    def serve(queries, found, out, put):
        spots, blocks = found
        lanes = lax.broadcasted_iota(jnp.int32, (SPAN, 128), 1)
        st = jnp.zeros((SPAN, 128), jnp.float32)
        zero = jnp.zeros((SPAN, DH), jnp.bfloat16)
        scores, vals = [], []
        for k in range(SLOTS):
            query = queries[spots[k]]
            keys = dbv[0, blocks[k]]
            vals.append(dbv[1, blocks[k]])
            for g in range(heads // 2):
                first = query[:, 2 * g * DH:(2 * g + 1) * DH]
                second = query[:, (2 * g + 1) * DH:(2 * g + 2) * DH]
                both = jnp.concatenate(
                    [jnp.concatenate([first, zero], axis=1), jnp.concatenate([zero, second], axis=1)], axis=0
                )
                scores.append(
                    lax.dot_general(
                        both, keys[:, 2 * g * DH:(2 * g + 2) * DH], NT, preferred_element_type=jnp.float32
                    )
                )
        s = jnp.concatenate(scores, axis=0)
        peak = jnp.max(s, axis=-1, keepdims=True)
        p = jnp.exp2((s - peak) * SCALE2)
        total = jnp.sum(p, axis=-1, keepdims=True)
        inv = 1.0 / total
        level = peak * SCALE2 + jnp.log(total) * LOG2E
        p = p.astype(jnp.bfloat16)
        for k in range(SLOTS):
            for g in range(heads // 2):
                n = k * heads + 2 * g
                o = jnp.dot(
                    p[n * SPAN:(n + 2) * SPAN], vals[k][:, 2 * g * DH:(2 * g + 2) * DH],
                    preferred_element_type=jnp.float32,
                )
                for e in (0, 1):
                    rs = slice((n + e) * SPAN, (n + e + 1) * SPAN)
                    part = o[e * SPAN:(e + 1) * SPAN, e * DH:(e + 1) * DH] * inv[rs]
                    out[k, :, (2 * g + e) * DH:(2 * g + e + 1) * DH] = part.astype(jnp.bfloat16)
                    st = jnp.where(lanes == n + e, level[rs], st)
        put[...] = st

    def serve_step(hop):
        for side in (0, 1):

            @pl.when(there(side, hop))
            def _():
                slot = (asker(side, hop) - d + n_d) % n_d
                found = lookups(lambda n: nbs[slot, 0, n])
                serve(cq_near[side][hop], found, osend.at[side, hop], stsend.at[side, hop])
                out_copy(side, hop).start()
                stat_copy(side, hop).start()

    def out_copy(side, hop):
        return remote(
            osend.at[side, hop], orecv.at[d], os_.at[side, hop], or_.at[d], db=asker(side, hop)
        )

    def stat_copy(side, hop):
        return remote(
            stsend.at[side, hop], strecv.at[d], ss.at[side, hop], sr.at[d], db=asker(side, hop)
        )

    def collect(owner):
        @pl.when(owner != d)
        def _():
            remote(osend.at[0, 0], orecv.at[owner], os_.at[0, 0], or_.at[owner], db=d).wait_recv()
            remote(stsend.at[0, 0], strecv.at[owner], ss.at[0, 0], sr.at[owner], db=d).wait_recv()

        packed = strecv[owner]
        stat[owner, 0] = packed
        for k in range(1, SLOTS):
            stat[owner, k] = pltpu.roll(packed, 128 - k * heads, 1)

    def combine():
        places = []
        owners = []
        for n in range(entries):
            owner = own_id(n) // PER_SHARD
            rank = jnp.int32(0)
            for earlier in owners:
                rank = rank + jnp.where(earlier == owner, 1, 0)
            owners.append(owner)
            places.append((jnp.clip(owner, 0, n_d - 1), jnp.minimum(rank, SLOTS - 1)))
        for u in range(spans):
            (oa, ka), (ob, kb) = places[2 * u], places[2 * u + 1]
            sa, sb = stat[oa, ka], stat[ob, kb]
            peak = jnp.maximum(sa, sb)
            ea = jnp.exp2(sa - peak)
            eb = jnp.exp2(sb - peak)
            inv = 1.0 / (ea + eb)
            ea, eb = ea * inv, eb * inv
            va, vb = orecv[oa, ka], orecv[ob, kb]
            for h in range(heads):
                hs = slice(h * DH, (h + 1) * DH)
                o = va[:, hs].astype(jnp.float32) * ea[:, h:h + 1] + vb[:, hs].astype(jnp.float32) * eb[:, h:h + 1]
                co[u * SPAN:(u + 1) * SPAN, hs] = o.astype(jnp.bfloat16)

    half_w = terms.shape[2]

    def project(rho, side):
        j = ((x + rho) % n_x - d + n_d) % n_d
        block = wg[:, j, :, side * half_w:(side + 1) * half_w].reshape(width, half_w)
        return jnp.dot(co[...], block, preferred_element_type=jnp.float32)

    rb_rows = rows // ROW_BLOCKS

    def ring_copy(side, step, rb):
        rs = pl.ds(rb * rb_rows, rb_rows)
        return remote(
            xsend.at[side, step, rs], xrecv.at[side, step, rs], xs.at[side, step, rb], xr.at[side, step, rb],
            tp=(right, left)[side],
        )

    def rho_of(side, step):
        return (n_x - 1 - step) % n_x if side == 0 else (1 + step) % n_x

    def ring_start():
        for side in (0, 1):
            xsend[side, 0] = project(rho_of(side, 0), side).astype(jnp.bfloat16)
            for rb in range(ROW_BLOCKS):
                ring_copy(side, 0, rb).start()
        for step in range(1, n_x):
            for side in (0, 1):
                terms[side * (n_x - 1) + step - 1] = project(rho_of(side, step), side)

    def ring_step(step):
        for rb in range(ROW_BLOCKS):
            rs = slice(rb * rb_rows, (rb + 1) * rb_rows)
            for side in (0, 1):
                ring_copy(side, step - 1, rb).wait_recv()
                total = xrecv[side, step - 1, rs].astype(jnp.float32) + terms[side * (n_x - 1) + step - 1, rs]
                xsend[side, step, rs] = total.astype(jnp.bfloat16)
                ring_copy(side, step, rb).start()

    def z_copy(rb):
        rs = pl.ds(rb * rb_rows, rb_rows)
        return remote(zsend.at[rs], zrecv.at[rs], zs.at[rb], zr.at[rb], tp=across)

    def ring_end():
        for rb in range(ROW_BLOCKS):
            rs = slice(rb * rb_rows, (rb + 1) * rb_rows)
            sums = []
            for side in (0, 1):
                ring_copy(side, n_x - 2, rb).wait_recv()
                sums.append(
                    xrecv[side, n_x - 2, rs].astype(jnp.float32) + terms[side * (n_x - 1) + n_x - 2, rs]
                )
            zsend[rs] = jnp.where(zh == 0, sums[1], sums[0]).astype(jnp.bfloat16)
            z_copy(rb).start()
            mine[rs] = jnp.where(zh == 0, sums[0], sums[1]) + hid[rs].astype(jnp.float32)

    def finish_self():
        for h in range(heads):
            hs = slice(h * DH, (h + 1) * DH)
            att_ref[:, hs] = (acc[h] / lref[h]).astype(jnp.bfloat16)

    for n in (3, 4):
        local[n].wait()
    serve(own_q, lookups(own_id), orecv.at[d], strecv.at[d])
    for j in range(1, n_d):
        remote(nbv.at[0], nbv.at[j], ns.at[j], nr.at[j], db=d).wait_recv()
        id_move(j).start()
    for n in (0, 1, 2):
        local[n].wait()
    attend_first()
    for j in range(1, n_d):
        id_move(j).wait()
    weight_step(0)
    query_step(0)
    serve_step(0)
    weight_step(1)
    query_step(1)
    serve_step(1)
    weight_step(2)
    advance(0, 0)
    query_step(2)
    serve_step(2)
    weight_step(3)
    advance(0, 1)
    pl.when(c == 1)(lambda: wait_passed(y))
    pl.when(c == 1)(lambda: attend(i - 1, 1))
    attend_step(0)
    advance(1, 0)
    weight_step(4)
    for owner in range(n_d):
        collect(owner)
    combine()
    weight_ready()
    local[5].wait()
    ring_start()
    advance(1, 1)
    attend_step(1)
    ring_step(1)
    advance(2, 0, 1)
    attend_step(2)
    ring_step(2)
    local[6].wait()
    ring_end()
    advance(3, 0, 1)
    attend_step(3)
    finish_self()
    for rb in range(ROW_BLOCKS):
        rs = slice(rb * rb_rows, (rb + 1) * rb_rows)
        z_copy(rb).wait_recv()
        mixed_ref[rs] = (mine[rs] + zrecv[rs].astype(jnp.float32)).astype(jnp.bfloat16)

    for m in range(1, n_d):
        id_copy(m).wait_send()
        weight_copy(m).wait_send()
    for side in (0, 1):
        for hop in range(hops):
            pl.when(query_goes(side, hop))(lambda side=side, hop=hop: query_copy(side, hop).wait_send())
            pl.when(there(side, hop))(lambda side=side, hop=hop: out_copy(side, hop).wait_send())
            pl.when(there(side, hop))(lambda side=side, hop=hop: stat_copy(side, hop).wait_send())
    for step in range(half):
        for part in (0, 1):
            if plus_has(step, part):
                pl.when(jnp.logical_and(y - step >= 0, y < n_y - 1))(
                    lambda step=step, part=part: plus_copy(step, part).wait_send())
            if minus_has(step, part):
                pl.when(minus_good((y + step) % n_y, part))(
                    lambda step=step, part=part: minus_copy(step, part).wait_send())
        wplus(step).wait_send()
        if step < half - 1:
            wminus(step).wait_send()
    for source in range(n_y):
        for part in (0, 1):
            pl.when(source < y)(lambda source=source, part=part: pass_copy(source, part, False).wait_send())
        wpass(source).wait_send()
    for part in (0, 1):
        pl.when(c == 0)(lambda part=part: pass_copy(y, part, True).wait_send())
    for side in (0, 1):
        for step in range(n_x - 1):
            for rb in range(ROW_BLOCKS):
                ring_copy(side, step, rb).wait_send()
    for rb in range(ROW_BLOCKS):
        z_copy(rb).wait_send()


def hand_over(a_ref, b_ref, a_out, b_out, sem):
    copies = [pltpu.make_async_copy(a_ref, a_out, sem.at[0]), pltpu.make_async_copy(b_ref, b_out, sem.at[1])]
    for copy in copies:
        copy.start()
    for copy in copies:
        copy.wait()


def shards(sizes, hidden_in, queries, keys, values, cross_queries, neighbours, database, out_weight):
    n_y, n_d, n_x = sizes
    half = n_y // 2
    rows, width = queries.shape[1:]
    heads = width // DH
    spans = rows // SPAN
    n_c = 2 * n_y
    piece = width // n_c
    cols = out_weight.shape[1]
    half_w = cols // 2
    bf16, f32 = jnp.bfloat16, jnp.float32
    vm, dma = pltpu.VMEM, pltpu.SemaphoreType.DMA
    any_spec = pl.BlockSpec(memory_space=pl.ANY)
    scratch = [vm((spans, SPAN, width), bf16) for _ in range(2 * n_d - 1)] + [
        vm((n_c, 2, rows, width), bf16),
        vm((rows, width), bf16),
        vm((rows, width), bf16),
        pltpu.SMEM((spans, NEIGH), jnp.int32),
        vm((n_d, 8, 128), jnp.int32),
        pltpu.SMEM((n_d, 8, 128), jnp.int32),
        vm(database.shape, bf16),
        vm((n_c, n_d, piece, cols), bf16),
        vm((2, n_d - 1, SLOTS, SPAN, width), bf16),
        vm((n_d, SLOTS, SPAN, width), bf16),
        vm((2, n_d - 1, SPAN, 128), f32),
        vm((n_d, SPAN, 128), f32),
        vm((n_d, SLOTS, SPAN, 128), f32),
        vm((rows, width), bf16),
        vm((2 * (n_x - 1), rows, half_w), f32),
        vm((2, n_x - 1, rows, half_w), bf16),
        vm((2, n_x - 1, rows, half_w), bf16),
        vm((rows, half_w), f32),
        vm((rows, half_w), bf16),
        vm((rows, half_w), bf16),
        vm((heads, rows, 1), f32),
        vm((heads, rows, 1), f32),
        vm((heads, rows, DH), f32),
        dma((8,)),
        dma((half, 2)), dma((half, 2)), dma((half, 2)), dma((half, 2)),
        dma((n_y, 2)), dma((n_y, 2)),
        dma((2, n_d - 1)), dma((2, n_d - 1)), dma((n_d,)), dma((n_d,)), dma((n_d,)),
        dma((2, n_d - 1)), dma((n_d,)), dma((2, n_d - 1)), dma((n_d,)),
        dma((n_d,)), dma((n_d,)),
        dma((half,)), dma((half,)), dma((half,)), dma((half,)),
        dma((n_y,)), dma((n_y,)),
        dma((2, n_x - 1, ROW_BLOCKS)), dma((2, n_x - 1, ROW_BLOCKS)),
        dma((ROW_BLOCKS,)), dma((ROW_BLOCKS,)),
    ]
    attended, mixed = pl.pallas_call(
        functools.partial(layer, sizes),
        out_shape=(
            jax.ShapeDtypeStruct((rows, width), bf16),
            jax.ShapeDtypeStruct((rows, half_w), bf16),
        ),
        in_specs=[any_spec] * 8,
        out_specs=(pl.BlockSpec(memory_space=pltpu.VMEM), pl.BlockSpec(memory_space=pltpu.VMEM)),
        scratch_shapes=scratch,
        compiler_params=pltpu.CompilerParams(
            collective_id=0, has_side_effects=True, vmem_limit_bytes=56 * 1024 * 1024
        ),
        name="layer",
    )(
        neighbours,
        hidden_in[0],
        queries[0],
        keys[0],
        values[0],
        cross_queries[0].reshape(spans, SPAN, width),
        database,
        out_weight.reshape(n_c, piece, cols),
    )
    attended, mixed = pl.pallas_call(
        hand_over,
        out_shape=(
            jax.ShapeDtypeStruct((rows, width), bf16),
            jax.ShapeDtypeStruct((rows, half_w), bf16),
        ),
        in_specs=[pl.BlockSpec(memory_space=pltpu.VMEM)] * 2,
        out_specs=(any_spec, any_spec),
        scratch_shapes=[dma((2,))],
        name="hand_over",
    )(attended, mixed)
    return attended[None], mixed[None]


def solution(mesh):
    sizes = (mesh.shape["ctx"] // 2, mesh.shape["db"], mesh.shape["tp"] // 2)
    in_specs = (
        P("db", "ctx", "tp"),
        P("db", "ctx", "tp"),
        P("db", "ctx", "tp"),
        P("db", "ctx", "tp"),
        P("db", "ctx", "tp"),
        P("db", "ctx", None),
        P(None, "db", None, "tp"),
        P("tp", "db"),
    )
    out_specs = (P("db", "ctx", "tp"), P("db", "ctx", "tp"))
    return jax.shard_map(
        functools.partial(shards, sizes), mesh=mesh, in_specs=in_specs, out_specs=out_specs, check_vma=False
    )
```

```python
import functools
import math

import jax
import jax.numpy as jnp
from jax import lax
from jax.experimental import pallas as pl
from jax.experimental.pallas import tpu as pltpu
from jax.sharding import PartitionSpec as P

DH = 128
SPAN = 64
NEIGH = 2
SLOTS = 4
PER_SHARD = 8
ROW_BLOCKS = 2
CUTS = 1
MESH = pl.DeviceIdType.MESH
SCALE = 1.0 / math.sqrt(DH)
SCALE2 = SCALE * math.log2(math.e)
LOG2E = math.log2(math.e)
NT = (((1,), (1,)), ((), ()))


def remote(src, dst, send_sem, recv_sem, **where):
    return pltpu.make_async_remote_copy(
        src_ref=src, dst_ref=dst, send_sem=send_sem, recv_sem=recv_sem, device_id=where, device_id_type=MESH
    )


def layer(sizes, near_hbm, hid_hbm, q_hbm, k_hbm, v_hbm, cq_hbm, db_hbm, w_hbm, att_ref, mixed_ref, *scratch):
    n_y, n_d, n_x = sizes
    half = n_y // 2
    (kv, qv, hid, near_ref, nbv, nbs, dbv, wg, osend, orecv_a, orecv_b, stsend, strecv, stat, co, terms, xsend, xrecv,
     mine, zsend, zrecv, mref, lref, acc,
     loc_sem, ps, pr, ms, mr, cs, cr, qs, qr, ns, nr, nl, os_, or_, ss, sr, wzs, wzr, wps, wpr, wms, wmr, wcs, wcr,
     xs, xr, zs, zr) = scratch[2 * n_d - 1:]
    hops = n_d - 1
    orecv_half = (orecv_a, orecv_b)
    own_q, cq_near = scratch[0], (scratch[1:n_d], scratch[n_d:2 * n_d - 1])
    rows = qv.shape[0]
    width = qv.shape[1]
    heads = width // DH
    cut = SPAN // ROW_BLOCKS
    rb_rows = rows // ROW_BLOCKS
    spans = rows // SPAN
    entries = spans * NEIGH

    i = lax.axis_index("ctx")
    d = lax.axis_index("db")
    t = lax.axis_index("tp")
    y, c = i // 2, i % 2
    x, zh = t // 2, t % 2
    other = i + 1 - 2 * c
    up = (i + 2) % (2 * n_y)
    down = (i + 2 * n_y - 2) % (2 * n_y)
    right = ((x + 1) % n_x) * 2 + zh
    left = ((x + n_x - 1) % n_x) * 2 + zh
    across = x * 2 + 1 - zh

    loads = [
        (q_hbm, qv), (k_hbm, kv.at[i, 0]), (v_hbm, kv.at[i, 1]), (cq_hbm, own_q),
        (db_hbm, dbv), (w_hbm, wg.at[:, 0]), (hid_hbm, hid), (near_hbm.at[0], near_ref),
    ]
    local = [pltpu.make_async_copy(a, b, loc_sem.at[n]) for n, (a, b) in enumerate(loads)]
    for n in (7, 3, 4, 0, 1, 2, 5, 6):
        local[n].start()
    barrier = pltpu.get_barrier_semaphore()
    greet = [dict(ctx=up), dict(ctx=down), dict(ctx=other), dict(tp=right), dict(tp=left), dict(tp=across)]
    greet += [dict(db=(d + m) % n_d) for m in range(1, n_d)]
    for where in greet:
        pl.semaphore_signal(barrier, inc=1, device_id=where, device_id_type=MESH)

    local[7].wait()
    lane = lax.broadcasted_iota(jnp.int32, (8, 128), 1)
    ids = jnp.zeros((8, 128), jnp.int32)
    for n in range(entries):
        ids = jnp.where(lane == n, near_ref[n // NEIGH, n % NEIGH], ids)
    nbv[0] = ids
    pl.semaphore_wait(barrier, len(greet))

    def id_copy(m):
        return remote(nbv.at[0], nbv.at[n_d - m], ns.at[n_d - m], nr.at[n_d - m], db=(d + m) % n_d)

    def there(side, hop):
        return d - 1 - hop >= 0 if side == 0 else d + 1 + hop < n_d

    def asker(side, hop):
        return d - 1 - hop if side == 0 else d + 1 + hop

    def query_copy(side, hop):
        src = cq_hbm if hop == 0 else cq_near[side][hop - 1]
        return remote(
            src, cq_near[side][hop], qs.at[side, hop], qr.at[side, hop], db=d + 1 - 2 * side
        )

    def query_goes(side, hop):
        if side == 0:
            return jnp.logical_and(d - hop >= 0, d < n_d - 1)
        return jnp.logical_and(d + hop < n_d, d > 0)

    def query_step(hop):
        for side in (0, 1):

            @pl.when(there(side, hop))
            def _():
                remote(cq_hbm, cq_near[side][hop], qs.at[side, hop], qr.at[side, hop], db=d).wait_recv()
                if hop + 1 < hops:
                    pl.when(query_goes(side, hop + 1))(lambda: query_copy(side, hop + 1).start())

    def weight_copy(m):
        j = n_d - m
        return remote(w_hbm.at[i], wg.at[i, j], wzs.at[j], wzr.at[j], db=(d + m) % n_d)

    def plus_has(step, part):
        return step < half - 1 or part == 0

    def plus_copy(step, part):
        slot = 2 * (y - step) + c
        src = (k_hbm, v_hbm)[part] if step == 0 else kv.at[slot, part]
        return remote(src, kv.at[slot, part], ps.at[step, part], pr.at[step, part], ctx=up)

    def minus_has(step, part):
        return part == 1 or step <= half - 2

    def minus_good(source, part):
        return source <= (half - 1 if part == 1 else half - 2)

    def minus_copy(step, part):
        slot = 2 * ((y + step) % n_y) + c
        src = (k_hbm, v_hbm)[part] if step == 0 else kv.at[slot, part]
        return remote(src, kv.at[slot, part], ms.at[step, part], mr.at[step, part], ctx=down)

    def pass_copy(source, part, own):
        slot = 2 * source + c
        src = (k_hbm, v_hbm)[part] if own else kv.at[slot, part]
        return remote(src, kv.at[slot, part], cs.at[source, part], cr.at[source, part], ctx=other)

    def kv_start(part):
        pl.when(y < n_y - 1)(lambda: plus_copy(0, part).start())
        pl.when(minus_good(y, part))(lambda: minus_copy(0, part).start())
        pl.when(c == 0)(lambda: pass_copy(y, part, True).start())

    for m in range(1, n_d):
        id_copy(m).start()
    for m in range(1, n_d):
        weight_copy(m).start()
    for side in (0, 1):
        pl.when(query_goes(side, 0))(lambda side=side: query_copy(side, 0).start())
    kv_start(0)
    kv_start(1)

    def head(h):
        return slice(h * DH, (h + 1) * DH)

    def attend_first():
        row = lax.broadcasted_iota(jnp.int32, (rows, rows), 0)
        col = lax.broadcasted_iota(jnp.int32, (rows, rows), 1)
        keep = col <= row
        scores = [
            lax.dot_general(qv[:, head(h)], kv[i, 0, :, head(h)], NT, preferred_element_type=jnp.float32)
            for h in range(heads)
        ]
        weights = []
        for h in range(heads):
            s = jnp.where(keep, scores[h], -1e30)
            peak = jnp.max(s, axis=-1, keepdims=True)
            p = jnp.exp2((s - peak) * SCALE2)
            mref[h] = peak
            lref[h] = jnp.sum(p, axis=-1, keepdims=True)
            weights.append(p.astype(jnp.bfloat16))
        for h in range(heads):
            acc[h] = jnp.dot(weights[h], kv[i, 1, :, head(h)], preferred_element_type=jnp.float32)

    def attend(start, count):
        for h in range(heads):
            keys = kv[pl.ds(start, count), 0, :, head(h)].reshape(count * rows, DH)
            vals = kv[pl.ds(start, count), 1, :, head(h)].reshape(count * rows, DH)
            for part in range(CUTS):
                rs = slice(part * rows // CUTS, (part + 1) * rows // CUTS)
                s = lax.dot_general(qv[rs, head(h)], keys, NT, preferred_element_type=jnp.float32)
                before = mref[h, rs]
                peak = jnp.maximum(before, jnp.max(s, axis=-1, keepdims=True))
                p = jnp.exp2((s - peak) * SCALE2)
                factor = jnp.exp2((before - peak) * SCALE2)
                mref[h, rs] = peak
                lref[h, rs] = lref[h, rs] * factor + jnp.sum(p, axis=-1, keepdims=True)
                fresh = jnp.dot(p.astype(jnp.bfloat16), vals, preferred_element_type=jnp.float32)
                acc[h, rs] = acc[h, rs] * factor + fresh

    def wait_passed(source):
        for part in (0, 1):
            slot = 2 * source + 1 - c
            remote(
                kv.at[slot, part], kv.at[slot, part], cs.at[source, part], cr.at[source, part], ctx=other
            ).wait_recv()

    def attend_pair(source):
        wait_passed(source)
        attend(2 * source, 2)

    def advance(step, *parts):
        for part in parts:
            if plus_has(step, part):
                source = y - 1 - step

                @pl.when(source >= 0)
                def _():
                    slot = 2 * source + c
                    remote(
                        kv.at[slot, part], kv.at[slot, part], ps.at[step, part], pr.at[step, part], ctx=up
                    ).wait_recv()
                    if step + 1 < half and plus_has(step + 1, part):
                        pl.when(y < n_y - 1)(lambda: plus_copy(step + 1, part).start())
                    pass_copy(source, part, False).start()

            if minus_has(step, part):
                source2 = (y + 1 + step) % n_y

                @pl.when(minus_good(source2, part))
                def _():
                    slot = 2 * source2 + c
                    remote(
                        kv.at[slot, part], kv.at[slot, part], ms.at[step, part], mr.at[step, part], ctx=down
                    ).wait_recv()
                    if step + 1 < half and minus_has(step + 1, part):
                        minus_copy(step + 1, part).start()
                    pl.when(source2 < y)(lambda: pass_copy(source2, part, False).start())

    def attend_step(step):
        if step < half - 1:
            pl.when(y - 1 - step >= 0)(lambda: attend_pair(y - 1 - step))
            pl.when(y + 1 + step >= n_y)(lambda: attend_pair(y + 1 + step - n_y))
        else:
            pl.when(y >= half)(lambda: attend_pair(y - half))

    def wplus(step):
        slot = 2 * ((y - step + n_y) % n_y) + c
        piece = wg.at[slot, pl.ds(1, n_d - 1)]
        return remote(piece, piece, wps.at[step], wpr.at[step], ctx=up)

    def wminus(step):
        slot = 2 * ((y + step) % n_y) + c
        piece = wg.at[slot, pl.ds(1, n_d - 1)]
        return remote(piece, piece, wms.at[step], wmr.at[step], ctx=down)

    def wpass(source):
        piece = wg.at[2 * source + c, pl.ds(1, n_d - 1)]
        return remote(piece, piece, wcs.at[source], wcr.at[source], ctx=other)

    def weight_step(step):
        if step == 0:
            for j in range(1, n_d):
                remote(w_hbm.at[i], wg.at[i, j], wzs.at[j], wzr.at[j], db=d).wait_recv()
            source = y
        else:
            source = (y - step + n_y) % n_y
            piece = wg.at[2 * source + c, pl.ds(1, n_d - 1)]
            remote(piece, piece, wps.at[step - 1], wpr.at[step - 1], ctx=up).wait_recv()
        if step < half:
            wplus(step).start()
        wpass(source).start()
        if step < half - 1 and step == 0:
            wminus(0).start()
        if 1 <= step <= half - 1:
            source2 = (y + step) % n_y
            piece2 = wg.at[2 * source2 + c, pl.ds(1, n_d - 1)]
            remote(piece2, piece2, wms.at[step - 1], wmr.at[step - 1], ctx=down).wait_recv()
            if step < half - 1:
                wminus(step).start()
            wpass(source2).start()

    def weight_ready():
        for source in range(n_y):
            piece = wg.at[2 * source + 1 - c, pl.ds(1, n_d - 1)]
            remote(piece, piece, wcs.at[source], wcr.at[source], ctx=other).wait_recv()

    def id_move(j):
        return pltpu.make_async_copy(nbv.at[j], nbs.at[j], nl.at[j])

    def lookups(block_id):
        spots = [jnp.int32(0)] * SLOTS
        blocks = [jnp.int32(0)] * SLOTS
        seen = jnp.int32(0)
        for n in range(entries):
            block = block_id(n)
            hit = (block // PER_SHARD) == d
            for k in range(min(n + 1, SLOTS)):
                take = jnp.logical_and(hit, seen == k)
                spots[k] = jnp.where(take, n // NEIGH, spots[k])
                blocks[k] = jnp.where(take, block % PER_SHARD, blocks[k])
            seen = seen + jnp.where(hit, 1, 0)
        return spots, blocks

    def own_id(n):
        return near_ref[n // NEIGH, n % NEIGH]

    def serve(queries, found, outs, put):
        spots, blocks = found
        lanes = lax.broadcasted_iota(jnp.int32, (SPAN, 128), 1)
        st = jnp.zeros((SPAN, 128), jnp.float32)
        zero = jnp.zeros((SPAN, DH), jnp.bfloat16)
        scores, vals = [], []
        for k in range(SLOTS):
            query = queries[spots[k]]
            keys = dbv[0, blocks[k]]
            vals.append(dbv[1, blocks[k]])
            for g in range(heads // 2):
                first = query[:, 2 * g * DH:(2 * g + 1) * DH]
                second = query[:, (2 * g + 1) * DH:(2 * g + 2) * DH]
                both = jnp.concatenate(
                    [jnp.concatenate([first, zero], axis=1), jnp.concatenate([zero, second], axis=1)], axis=0
                )
                scores.append(
                    lax.dot_general(
                        both, keys[:, 2 * g * DH:(2 * g + 2) * DH], NT, preferred_element_type=jnp.float32
                    )
                )
        s = jnp.concatenate(scores, axis=0)
        peak = jnp.max(s, axis=-1, keepdims=True)
        p = jnp.exp2((s - peak) * SCALE2)
        total = jnp.sum(p, axis=-1, keepdims=True)
        inv = 1.0 / total
        level = peak * SCALE2 + jnp.log(total) * LOG2E
        p = p.astype(jnp.bfloat16)
        for k in range(SLOTS):
            for g in range(heads // 2):
                n = k * heads + 2 * g
                o = jnp.dot(
                    p[n * SPAN:(n + 2) * SPAN], vals[k][:, 2 * g * DH:(2 * g + 2) * DH],
                    preferred_element_type=jnp.float32,
                )
                for e in (0, 1):
                    rs = slice((n + e) * SPAN, (n + e + 1) * SPAN)
                    part = o[e * SPAN:(e + 1) * SPAN, e * DH:(e + 1) * DH] * inv[rs]
                    for rb in range(ROW_BLOCKS):
                        outs[rb][k, :, (2 * g + e) * DH:(2 * g + e + 1) * DH] = part[
                            rb * cut:(rb + 1) * cut
                        ].astype(jnp.bfloat16)
                    st = jnp.where(lanes == n + e, level[rs], st)
        put[...] = st

    def serve_step(hop):
        for side in (0, 1):

            @pl.when(there(side, hop))
            def _():
                slot = (asker(side, hop) - d + n_d) % n_d
                found = lookups(lambda n: nbs[slot, 0, n])
                serve(
                    cq_near[side][hop], found, [osend.at[side, hop, rb] for rb in range(ROW_BLOCKS)],
                    stsend.at[side, hop],
                )
                out_copy(side, hop, 0).start()
                stat_copy(side, hop).start()

    def later_half(hop):
        for side in (0, 1):
            pl.when(there(side, hop))(lambda side=side: out_copy(side, hop, 1).start())

    def out_copy(side, hop, rb):
        return remote(
            osend.at[side, hop, rb], orecv_half[rb].at[d], os_.at[side, hop, rb], or_.at[d, rb], db=asker(side, hop)
        )

    def stat_copy(side, hop):
        return remote(
            stsend.at[side, hop], strecv.at[d], ss.at[side, hop], sr.at[d], db=asker(side, hop)
        )

    def collect(owner, rb):
        @pl.when(owner != d)
        def _():
            remote(
                osend.at[0, 0, rb], orecv_half[rb].at[owner], os_.at[0, 0, rb], or_.at[owner, rb], db=d
            ).wait_recv()
            if rb == 0:
                remote(stsend.at[0, 0], strecv.at[owner], ss.at[0, 0], sr.at[owner], db=d).wait_recv()

        if rb == 0:
            packed = strecv[owner]
            stat[owner, 0] = packed
            for k in range(1, SLOTS):
                stat[owner, k] = pltpu.roll(packed, 128 - k * heads, 1)

    def combine(rb):
        places = []
        owners = []
        for n in range(entries):
            owner = own_id(n) // PER_SHARD
            rank = jnp.int32(0)
            for earlier in owners:
                rank = rank + jnp.where(earlier == owner, 1, 0)
            owners.append(owner)
            places.append((jnp.clip(owner, 0, n_d - 1), jnp.minimum(rank, SLOTS - 1)))
        for u in range(spans):
            (oa, ka), (ob, kb) = places[2 * u], places[2 * u + 1]
            half_rows = pl.ds(rb * cut, cut)
            sa, sb = stat[oa, ka, half_rows], stat[ob, kb, half_rows]
            peak = jnp.maximum(sa, sb)
            ea = jnp.exp2(sa - peak)
            eb = jnp.exp2(sb - peak)
            inv = 1.0 / (ea + eb)
            ea, eb = ea * inv, eb * inv
            va, vb = orecv_half[rb][oa, ka], orecv_half[rb][ob, kb]
            for h in range(heads):
                hs = slice(h * DH, (h + 1) * DH)
                o = va[:, hs].astype(jnp.float32) * ea[:, h:h + 1] + vb[:, hs].astype(jnp.float32) * eb[:, h:h + 1]
                co[rb * rb_rows + u * cut:rb * rb_rows + (u + 1) * cut, hs] = o.astype(jnp.bfloat16)

    half_w = terms.shape[2]

    def project(rho, side, rb):
        j = ((x + rho) % n_x - d + n_d) % n_d
        block = wg[:, j, :, side * half_w:(side + 1) * half_w].reshape(width, half_w)
        return jnp.dot(co[rb * rb_rows:(rb + 1) * rb_rows], block, preferred_element_type=jnp.float32)


    def ring_copy(side, step, rb):
        rs = pl.ds(rb * rb_rows, rb_rows)
        return remote(
            xsend.at[side, step, rs], xrecv.at[side, step, rs], xs.at[side, step, rb], xr.at[side, step, rb],
            tp=(right, left)[side],
        )

    def rho_of(side, step):
        return (n_x - 1 - step) % n_x if side == 0 else (1 + step) % n_x

    def ring_start(rb):
        rs = slice(rb * rb_rows, (rb + 1) * rb_rows)
        for side in (0, 1):
            xsend[side, 0, rs] = project(rho_of(side, 0), side, rb).astype(jnp.bfloat16)
            ring_copy(side, 0, rb).start()
        for step in range(1, n_x):
            for side in (0, 1):
                terms[side * (n_x - 1) + step - 1, rs] = project(rho_of(side, step), side, rb)

    def ring_step(step, rb):
        rs = slice(rb * rb_rows, (rb + 1) * rb_rows)
        for side in (0, 1):
            ring_copy(side, step - 1, rb).wait_recv()
            total = xrecv[side, step - 1, rs].astype(jnp.float32) + terms[side * (n_x - 1) + step - 1, rs]
            xsend[side, step, rs] = total.astype(jnp.bfloat16)
            ring_copy(side, step, rb).start()

    def z_copy(rb):
        rs = pl.ds(rb * rb_rows, rb_rows)
        return remote(zsend.at[rs], zrecv.at[rs], zs.at[rb], zr.at[rb], tp=across)

    def span_rows(u, rb):
        return slice(u * SPAN + rb * cut, u * SPAN + (rb + 1) * cut)

    def ring_end(rb):
        rs = slice(rb * rb_rows, (rb + 1) * rb_rows)
        sums = []
        for side in (0, 1):
            ring_copy(side, n_x - 2, rb).wait_recv()
            sums.append(xrecv[side, n_x - 2, rs].astype(jnp.float32) + terms[side * (n_x - 1) + n_x - 2, rs])
        zsend[rs] = jnp.where(zh == 0, sums[1], sums[0]).astype(jnp.bfloat16)
        z_copy(rb).start()
        before = jnp.concatenate([hid[span_rows(u, rb)] for u in range(spans)], axis=0)
        mine[rs] = jnp.where(zh == 0, sums[0], sums[1]) + before.astype(jnp.float32)

    def finish_self():
        for h in range(heads):
            hs = slice(h * DH, (h + 1) * DH)
            att_ref[:, hs] = (acc[h] / lref[h]).astype(jnp.bfloat16)

    for n in (3, 4):
        local[n].wait()
    serve(own_q, lookups(own_id), [ref.at[d] for ref in orecv_half], strecv.at[d])
    for j in range(1, n_d):
        remote(nbv.at[0], nbv.at[j], ns.at[j], nr.at[j], db=d).wait_recv()
        id_move(j).start()
    for n in (0, 1, 2):
        local[n].wait()
    attend_first()
    for j in range(1, n_d):
        id_move(j).wait()
    weight_step(0)
    query_step(0)
    serve_step(0)
    weight_step(1)
    query_step(1)
    serve_step(1)
    later_half(0)
    weight_step(2)
    advance(0, 0)
    query_step(2)
    serve_step(2)
    later_half(1)
    later_half(2)
    weight_step(3)
    advance(0, 1)
    pl.when(c == 1)(lambda: wait_passed(y))
    pl.when(c == 1)(lambda: attend(i - 1, 1))
    attend_step(0)
    advance(1, 0)
    weight_step(4)
    for owner in range(n_d):
        collect(owner, 0)
    combine(0)
    weight_ready()
    local[5].wait()
    ring_start(0)
    advance(1, 1)
    for owner in range(n_d):
        collect(owner, 1)
    combine(1)
    ring_step(1, 0)
    ring_start(1)
    attend_step(1)
    ring_step(2, 0)
    ring_step(1, 1)
    local[6].wait()
    ring_end(0)
    advance(2, 0, 1)
    ring_step(2, 1)
    attend_step(2)
    ring_end(1)
    advance(3, 0, 1)
    attend_step(3)
    finish_self()
    for rb in range(ROW_BLOCKS):
        rs = slice(rb * rb_rows, (rb + 1) * rb_rows)
        z_copy(rb).wait_recv()
        whole = (mine[rs] + zrecv[rs].astype(jnp.float32)).astype(jnp.bfloat16)
        for u in range(spans):
            mixed_ref[span_rows(u, rb)] = whole[u * cut:(u + 1) * cut]

    for m in range(1, n_d):
        id_copy(m).wait_send()
        weight_copy(m).wait_send()
    for side in (0, 1):
        for hop in range(hops):
            pl.when(query_goes(side, hop))(lambda side=side, hop=hop: query_copy(side, hop).wait_send())
            pl.when(there(side, hop))(lambda side=side, hop=hop: [out_copy(side, hop, rb).wait_send() for rb in range(ROW_BLOCKS)] and None)
            pl.when(there(side, hop))(lambda side=side, hop=hop: stat_copy(side, hop).wait_send())
    for step in range(half):
        for part in (0, 1):
            if plus_has(step, part):
                pl.when(jnp.logical_and(y - step >= 0, y < n_y - 1))(
                    lambda step=step, part=part: plus_copy(step, part).wait_send())
            if minus_has(step, part):
                pl.when(minus_good((y + step) % n_y, part))(
                    lambda step=step, part=part: minus_copy(step, part).wait_send())
        wplus(step).wait_send()
        if step < half - 1:
            wminus(step).wait_send()
    for source in range(n_y):
        for part in (0, 1):
            pl.when(source < y)(lambda source=source, part=part: pass_copy(source, part, False).wait_send())
        wpass(source).wait_send()
    for part in (0, 1):
        pl.when(c == 0)(lambda part=part: pass_copy(y, part, True).wait_send())
    for side in (0, 1):
        for step in range(n_x - 1):
            for rb in range(ROW_BLOCKS):
                ring_copy(side, step, rb).wait_send()
    for rb in range(ROW_BLOCKS):
        z_copy(rb).wait_send()


def hand_over(a_ref, b_ref, a_out, b_out, sem):
    copies = [pltpu.make_async_copy(a_ref, a_out, sem.at[0]), pltpu.make_async_copy(b_ref, b_out, sem.at[1])]
    for copy in copies:
        copy.start()
    for copy in copies:
        copy.wait()


def shards(sizes, hidden_in, queries, keys, values, cross_queries, neighbours, database, out_weight):
    n_y, n_d, n_x = sizes
    half = n_y // 2
    rows, width = queries.shape[1:]
    heads = width // DH
    spans = rows // SPAN
    n_c = 2 * n_y
    piece = width // n_c
    cols = out_weight.shape[1]
    half_w = cols // 2
    bf16, f32 = jnp.bfloat16, jnp.float32
    vm, dma = pltpu.VMEM, pltpu.SemaphoreType.DMA
    any_spec = pl.BlockSpec(memory_space=pl.ANY)
    scratch = [vm((spans, SPAN, width), bf16) for _ in range(2 * n_d - 1)] + [
        vm((n_c, 2, rows, width), bf16),
        vm((rows, width), bf16),
        vm((rows, width), bf16),
        pltpu.SMEM((spans, NEIGH), jnp.int32),
        vm((n_d, 8, 128), jnp.int32),
        pltpu.SMEM((n_d, 8, 128), jnp.int32),
        vm(database.shape, bf16),
        vm((n_c, n_d, piece, cols), bf16),
        vm((2, n_d - 1, ROW_BLOCKS, SLOTS, SPAN // ROW_BLOCKS, width), bf16),
        vm((n_d, SLOTS, SPAN // ROW_BLOCKS, width), bf16),
        vm((n_d, SLOTS, SPAN // ROW_BLOCKS, width), bf16),
        vm((2, n_d - 1, SPAN, 128), f32),
        vm((n_d, SPAN, 128), f32),
        vm((n_d, SLOTS, SPAN, 128), f32),
        vm((rows, width), bf16),
        vm((2 * (n_x - 1), rows, half_w), f32),
        vm((2, n_x - 1, rows, half_w), bf16),
        vm((2, n_x - 1, rows, half_w), bf16),
        vm((rows, half_w), f32),
        vm((rows, half_w), bf16),
        vm((rows, half_w), bf16),
        vm((heads, rows, 1), f32),
        vm((heads, rows, 1), f32),
        vm((heads, rows, DH), f32),
        dma((8,)),
        dma((half, 2)), dma((half, 2)), dma((half, 2)), dma((half, 2)),
        dma((n_y, 2)), dma((n_y, 2)),
        dma((2, n_d - 1)), dma((2, n_d - 1)), dma((n_d,)), dma((n_d,)), dma((n_d,)),
        dma((2, n_d - 1, ROW_BLOCKS)), dma((n_d, ROW_BLOCKS)), dma((2, n_d - 1)), dma((n_d,)),
        dma((n_d,)), dma((n_d,)),
        dma((half,)), dma((half,)), dma((half,)), dma((half,)),
        dma((n_y,)), dma((n_y,)),
        dma((2, n_x - 1, ROW_BLOCKS)), dma((2, n_x - 1, ROW_BLOCKS)),
        dma((ROW_BLOCKS,)), dma((ROW_BLOCKS,)),
    ]
    attended, mixed = pl.pallas_call(
        functools.partial(layer, sizes),
        out_shape=(
            jax.ShapeDtypeStruct((rows, width), bf16),
            jax.ShapeDtypeStruct((rows, half_w), bf16),
        ),
        in_specs=[any_spec] * 8,
        out_specs=(pl.BlockSpec(memory_space=pltpu.VMEM), pl.BlockSpec(memory_space=pltpu.VMEM)),
        scratch_shapes=scratch,
        compiler_params=pltpu.CompilerParams(
            collective_id=0, has_side_effects=True, vmem_limit_bytes=56 * 1024 * 1024
        ),
        name="layer",
    )(
        neighbours,
        hidden_in[0],
        queries[0],
        keys[0],
        values[0],
        cross_queries[0].reshape(spans, SPAN, width),
        database,
        out_weight.reshape(n_c, piece, cols),
    )
    attended, mixed = pl.pallas_call(
        hand_over,
        out_shape=(
            jax.ShapeDtypeStruct((rows, width), bf16),
            jax.ShapeDtypeStruct((rows, half_w), bf16),
        ),
        in_specs=[pl.BlockSpec(memory_space=pltpu.VMEM)] * 2,
        out_specs=(any_spec, any_spec),
        scratch_shapes=[dma((2,))],
        name="hand_over",
    )(attended, mixed)
    return attended[None], mixed[None]


def solution(mesh):
    sizes = (mesh.shape["ctx"] // 2, mesh.shape["db"], mesh.shape["tp"] // 2)
    in_specs = (
        P("db", "ctx", "tp"),
        P("db", "ctx", "tp"),
        P("db", "ctx", "tp"),
        P("db", "ctx", "tp"),
        P("db", "ctx", "tp"),
        P("db", "ctx", None),
        P(None, "db", None, "tp"),
        P("tp", "db"),
    )
    out_specs = (P("db", "ctx", "tp"), P("db", "ctx", "tp"))
    return jax.shard_map(
        functools.partial(shards, sizes), mesh=mesh, in_specs=in_specs, out_specs=out_specs, check_vma=False
    )
```

```python
import functools
import math

import jax
import jax.numpy as jnp
from jax import lax
from jax.experimental import pallas as pl
from jax.experimental.pallas import tpu as pltpu
from jax.sharding import PartitionSpec as P

DH = 128
SPAN = 64
NEIGH = 2
SLOTS = 4
PER_SHARD = 8
ROW_BLOCKS = 2
CUTS = 1
MESH = pl.DeviceIdType.MESH
SCALE = 1.0 / math.sqrt(DH)
SCALE2 = SCALE * math.log2(math.e)
LOG2E = math.log2(math.e)
NT = (((1,), (1,)), ((), ()))


def remote(src, dst, send_sem, recv_sem, **where):
    return pltpu.make_async_remote_copy(
        src_ref=src, dst_ref=dst, send_sem=send_sem, recv_sem=recv_sem, device_id=where, device_id_type=MESH
    )


def layer(sizes, near_hbm, hid_hbm, q_hbm, k_hbm, v_hbm, cq_hbm, db_hbm, w_hbm, att_ref, mixed_ref, *scratch):
    n_y, n_d, n_x = sizes
    half = n_y // 2
    (kv, qv, hid, near_ref, nbv, nbs, dbv, wg, osend, orecv_a, orecv_b, stsend, strecv, stat, co, terms, xsend, xrecv,
     mine, zsend, zrecv, mref, lref, acc,
     loc_sem, ps, pr, ms, mr, cs, cr, qs, qr, ns, nr, nl, os_, or_, ss, sr, wzs, wzr, wps, wpr, wms, wmr, wcs, wcr,
     xs, xr, zs, zr) = scratch[2 * n_d - 1:]
    hops = n_d - 1
    orecv_half = (orecv_a, orecv_b)
    own_q, cq_near = scratch[0], (scratch[1:n_d], scratch[n_d:2 * n_d - 1])
    rows = qv.shape[0]
    width = qv.shape[1]
    heads = width // DH
    cut = SPAN // ROW_BLOCKS
    rb_rows = rows // ROW_BLOCKS
    spans = rows // SPAN
    entries = spans * NEIGH

    i = lax.axis_index("ctx")
    d = lax.axis_index("db")
    t = lax.axis_index("tp")
    y, c = i // 2, i % 2
    x, zh = t // 2, t % 2
    other = i + 1 - 2 * c
    up = (i + 2) % (2 * n_y)
    down = (i + 2 * n_y - 2) % (2 * n_y)
    right = ((x + 1) % n_x) * 2 + zh
    left = ((x + n_x - 1) % n_x) * 2 + zh
    across = x * 2 + 1 - zh

    loads = [
        (q_hbm, qv), (k_hbm, kv.at[i, 0]), (v_hbm, kv.at[i, 1]), (cq_hbm, own_q),
        (db_hbm, dbv), (w_hbm, wg.at[:, 0]), (hid_hbm, hid), (near_hbm.at[0], near_ref),
    ]
    local = [pltpu.make_async_copy(a, b, loc_sem.at[n]) for n, (a, b) in enumerate(loads)]
    for n in (7, 3, 4, 0, 1, 2, 5, 6):
        local[n].start()
    barrier = pltpu.get_barrier_semaphore()
    greet = [dict(ctx=up), dict(ctx=down), dict(ctx=other), dict(tp=right), dict(tp=left), dict(tp=across)]
    greet += [dict(db=(d + m) % n_d) for m in range(1, n_d)]
    for where in greet:
        pl.semaphore_signal(barrier, inc=1, device_id=where, device_id_type=MESH)

    local[7].wait()
    lane = lax.broadcasted_iota(jnp.int32, (8, 128), 1)
    ids = jnp.zeros((8, 128), jnp.int32)
    for n in range(entries):
        ids = jnp.where(lane == n, near_ref[n // NEIGH, n % NEIGH], ids)
    nbv[0] = ids
    pl.semaphore_wait(barrier, len(greet))

    def id_copy(m):
        return remote(nbv.at[0], nbv.at[n_d - m], ns.at[n_d - m], nr.at[n_d - m], db=(d + m) % n_d)

    def there(side, hop):
        return d - 1 - hop >= 0 if side == 0 else d + 1 + hop < n_d

    def asker(side, hop):
        return d - 1 - hop if side == 0 else d + 1 + hop

    def query_copy(side, hop):
        src = cq_hbm if hop == 0 else cq_near[side][hop - 1]
        return remote(
            src, cq_near[side][hop], qs.at[side, hop], qr.at[side, hop], db=d + 1 - 2 * side
        )

    def query_goes(side, hop):
        if side == 0:
            return jnp.logical_and(d - hop >= 0, d < n_d - 1)
        return jnp.logical_and(d + hop < n_d, d > 0)

    def query_step(hop):
        for side in (0, 1):

            @pl.when(there(side, hop))
            def _():
                remote(cq_hbm, cq_near[side][hop], qs.at[side, hop], qr.at[side, hop], db=d).wait_recv()
                if hop + 1 < hops:
                    pl.when(query_goes(side, hop + 1))(lambda: query_copy(side, hop + 1).start())

    def weight_copy(m):
        j = n_d - m
        return remote(w_hbm.at[i], wg.at[i, j], wzs.at[j], wzr.at[j], db=(d + m) % n_d)

    def plus_has(step, part):
        return step < half - 1 or part == 0

    def plus_copy(step, part):
        slot = 2 * (y - step) + c
        src = (k_hbm, v_hbm)[part] if step == 0 else kv.at[slot, part]
        return remote(src, kv.at[slot, part], ps.at[step, part], pr.at[step, part], ctx=up)

    def minus_has(step, part):
        return part == 1 or step <= half - 2

    def minus_good(source, part):
        return source <= (half - 1 if part == 1 else half - 2)

    def minus_copy(step, part):
        slot = 2 * ((y + step) % n_y) + c
        src = (k_hbm, v_hbm)[part] if step == 0 else kv.at[slot, part]
        return remote(src, kv.at[slot, part], ms.at[step, part], mr.at[step, part], ctx=down)

    def pass_copy(source, part, own):
        slot = 2 * source + c
        src = (k_hbm, v_hbm)[part] if own else kv.at[slot, part]
        return remote(src, kv.at[slot, part], cs.at[source, part], cr.at[source, part], ctx=other)

    def kv_start(part):
        pl.when(y < n_y - 1)(lambda: plus_copy(0, part).start())
        pl.when(minus_good(y, part))(lambda: minus_copy(0, part).start())
        pl.when(c == 0)(lambda: pass_copy(y, part, True).start())

    for m in range(1, n_d):
        id_copy(m).start()
    for m in range(1, n_d):
        weight_copy(m).start()
    for side in (0, 1):
        pl.when(query_goes(side, 0))(lambda side=side: query_copy(side, 0).start())
    kv_start(0)

    def head(h):
        return slice(h * DH, (h + 1) * DH)

    def attend_first():
        row = lax.broadcasted_iota(jnp.int32, (rows, rows), 0)
        col = lax.broadcasted_iota(jnp.int32, (rows, rows), 1)
        keep = col <= row
        scores = [
            lax.dot_general(qv[:, head(h)], kv[i, 0, :, head(h)], NT, preferred_element_type=jnp.float32)
            for h in range(heads)
        ]
        weights = []
        for h in range(heads):
            s = jnp.where(keep, scores[h], -1e30)
            peak = jnp.max(s, axis=-1, keepdims=True)
            p = jnp.exp2((s - peak) * SCALE2)
            mref[h] = peak
            lref[h] = jnp.sum(p, axis=-1, keepdims=True)
            weights.append(p.astype(jnp.bfloat16))
        for h in range(heads):
            acc[h] = jnp.dot(weights[h], kv[i, 1, :, head(h)], preferred_element_type=jnp.float32)

    def attend(start, count):
        for h in range(heads):
            keys = kv[pl.ds(start, count), 0, :, head(h)].reshape(count * rows, DH)
            vals = kv[pl.ds(start, count), 1, :, head(h)].reshape(count * rows, DH)
            for part in range(CUTS):
                rs = slice(part * rows // CUTS, (part + 1) * rows // CUTS)
                s = lax.dot_general(qv[rs, head(h)], keys, NT, preferred_element_type=jnp.float32)
                before = mref[h, rs]
                peak = jnp.maximum(before, jnp.max(s, axis=-1, keepdims=True))
                p = jnp.exp2((s - peak) * SCALE2)
                factor = jnp.exp2((before - peak) * SCALE2)
                mref[h, rs] = peak
                lref[h, rs] = lref[h, rs] * factor + jnp.sum(p, axis=-1, keepdims=True)
                fresh = jnp.dot(p.astype(jnp.bfloat16), vals, preferred_element_type=jnp.float32)
                acc[h, rs] = acc[h, rs] * factor + fresh

    def wait_passed(source):
        for part in (0, 1):
            slot = 2 * source + 1 - c
            remote(
                kv.at[slot, part], kv.at[slot, part], cs.at[source, part], cr.at[source, part], ctx=other
            ).wait_recv()

    def attend_pair(source):
        wait_passed(source)
        attend(2 * source, 2)

    def advance(step, *parts):
        for part in parts:
            if plus_has(step, part):
                source = y - 1 - step

                @pl.when(source >= 0)
                def _():
                    slot = 2 * source + c
                    remote(
                        kv.at[slot, part], kv.at[slot, part], ps.at[step, part], pr.at[step, part], ctx=up
                    ).wait_recv()
                    if step + 1 < half and plus_has(step + 1, part):
                        pl.when(y < n_y - 1)(lambda: plus_copy(step + 1, part).start())
                    pass_copy(source, part, False).start()

            if minus_has(step, part):
                source2 = (y + 1 + step) % n_y

                @pl.when(minus_good(source2, part))
                def _():
                    slot = 2 * source2 + c
                    remote(
                        kv.at[slot, part], kv.at[slot, part], ms.at[step, part], mr.at[step, part], ctx=down
                    ).wait_recv()
                    if step + 1 < half and minus_has(step + 1, part):
                        minus_copy(step + 1, part).start()
                    pl.when(source2 < y)(lambda: pass_copy(source2, part, False).start())

    def attend_step(step):
        if step < half - 1:
            pl.when(y - 1 - step >= 0)(lambda: attend_pair(y - 1 - step))
            pl.when(y + 1 + step >= n_y)(lambda: attend_pair(y + 1 + step - n_y))
        else:
            pl.when(y >= half)(lambda: attend_pair(y - half))

    def wplus(step):
        slot = 2 * ((y - step + n_y) % n_y) + c
        piece = wg.at[slot, pl.ds(1, n_d - 1)]
        return remote(piece, piece, wps.at[step], wpr.at[step], ctx=up)

    def wminus(step):
        slot = 2 * ((y + step) % n_y) + c
        piece = wg.at[slot, pl.ds(1, n_d - 1)]
        return remote(piece, piece, wms.at[step], wmr.at[step], ctx=down)

    def wpass(source):
        piece = wg.at[2 * source + c, pl.ds(1, n_d - 1)]
        return remote(piece, piece, wcs.at[source], wcr.at[source], ctx=other)

    def weight_step(step):
        if step == 0:
            for j in range(1, n_d):
                remote(w_hbm.at[i], wg.at[i, j], wzs.at[j], wzr.at[j], db=d).wait_recv()
            source = y
        else:
            source = (y - step + n_y) % n_y
            piece = wg.at[2 * source + c, pl.ds(1, n_d - 1)]
            remote(piece, piece, wps.at[step - 1], wpr.at[step - 1], ctx=up).wait_recv()
        if step < half:
            wplus(step).start()
        wpass(source).start()
        if step < half - 1 and step == 0:
            wminus(0).start()
        if 1 <= step <= half - 1:
            source2 = (y + step) % n_y
            piece2 = wg.at[2 * source2 + c, pl.ds(1, n_d - 1)]
            remote(piece2, piece2, wms.at[step - 1], wmr.at[step - 1], ctx=down).wait_recv()
            if step < half - 1:
                wminus(step).start()
            wpass(source2).start()

    def weight_ready():
        for source in range(n_y):
            piece = wg.at[2 * source + 1 - c, pl.ds(1, n_d - 1)]
            remote(piece, piece, wcs.at[source], wcr.at[source], ctx=other).wait_recv()

    def id_move(j):
        return pltpu.make_async_copy(nbv.at[j], nbs.at[j], nl.at[j])

    def lookups(block_id):
        spots = [jnp.int32(0)] * SLOTS
        blocks = [jnp.int32(0)] * SLOTS
        seen = jnp.int32(0)
        for n in range(entries):
            block = block_id(n)
            hit = (block // PER_SHARD) == d
            for k in range(min(n + 1, SLOTS)):
                take = jnp.logical_and(hit, seen == k)
                spots[k] = jnp.where(take, n // NEIGH, spots[k])
                blocks[k] = jnp.where(take, block % PER_SHARD, blocks[k])
            seen = seen + jnp.where(hit, 1, 0)
        return spots, blocks

    def own_id(n):
        return near_ref[n // NEIGH, n % NEIGH]

    def serve(queries, found, outs, put):
        spots, blocks = found
        lanes = lax.broadcasted_iota(jnp.int32, (SPAN, 128), 1)
        st = jnp.zeros((SPAN, 128), jnp.float32)
        zero = jnp.zeros((SPAN, DH), jnp.bfloat16)
        scores, vals = [], []
        for k in range(SLOTS):
            query = queries[spots[k]]
            keys = dbv[0, blocks[k]]
            vals.append(dbv[1, blocks[k]])
            for g in range(heads // 2):
                first = query[:, 2 * g * DH:(2 * g + 1) * DH]
                second = query[:, (2 * g + 1) * DH:(2 * g + 2) * DH]
                both = jnp.concatenate(
                    [jnp.concatenate([first, zero], axis=1), jnp.concatenate([zero, second], axis=1)], axis=0
                )
                scores.append(
                    lax.dot_general(
                        both, keys[:, 2 * g * DH:(2 * g + 2) * DH], NT, preferred_element_type=jnp.float32
                    )
                )
        s = jnp.concatenate(scores, axis=0)
        peak = jnp.max(s, axis=-1, keepdims=True)
        p = jnp.exp2((s - peak) * SCALE2)
        total = jnp.sum(p, axis=-1, keepdims=True)
        inv = 1.0 / total
        level = peak * SCALE2 + jnp.log(total) * LOG2E
        p = p.astype(jnp.bfloat16)
        for k in range(SLOTS):
            for g in range(heads // 2):
                n = k * heads + 2 * g
                o = jnp.dot(
                    p[n * SPAN:(n + 2) * SPAN], vals[k][:, 2 * g * DH:(2 * g + 2) * DH],
                    preferred_element_type=jnp.float32,
                )
                for e in (0, 1):
                    rs = slice((n + e) * SPAN, (n + e + 1) * SPAN)
                    part = o[e * SPAN:(e + 1) * SPAN, e * DH:(e + 1) * DH] * inv[rs]
                    for rb in range(ROW_BLOCKS):
                        outs[rb][k, :, (2 * g + e) * DH:(2 * g + e + 1) * DH] = part[
                            rb * cut:(rb + 1) * cut
                        ].astype(jnp.bfloat16)
                    st = jnp.where(lanes == n + e, level[rs], st)
        put[...] = st

    def serve_step(hop):
        for side in (0, 1):

            @pl.when(there(side, hop))
            def _():
                slot = (asker(side, hop) - d + n_d) % n_d
                found = lookups(lambda n: nbs[slot, 0, n])
                serve(
                    cq_near[side][hop], found, [osend.at[side, hop, rb] for rb in range(ROW_BLOCKS)],
                    stsend.at[side, hop],
                )
                out_copy(side, hop, 0).start()
                stat_copy(side, hop).start()

    def later_half(hop):
        for side in (0, 1):
            pl.when(there(side, hop))(lambda side=side: out_copy(side, hop, 1).start())

    def out_copy(side, hop, rb):
        return remote(
            osend.at[side, hop, rb], orecv_half[rb].at[d], os_.at[side, hop, rb], or_.at[d, rb], db=asker(side, hop)
        )

    def stat_copy(side, hop):
        return remote(
            stsend.at[side, hop], strecv.at[d], ss.at[side, hop], sr.at[d], db=asker(side, hop)
        )

    def collect(owner, rb):
        @pl.when(owner != d)
        def _():
            remote(
                osend.at[0, 0, rb], orecv_half[rb].at[owner], os_.at[0, 0, rb], or_.at[owner, rb], db=d
            ).wait_recv()
            if rb == 0:
                remote(stsend.at[0, 0], strecv.at[owner], ss.at[0, 0], sr.at[owner], db=d).wait_recv()

        if rb == 0:
            packed = strecv[owner]
            stat[owner, 0] = packed
            for k in range(1, SLOTS):
                stat[owner, k] = pltpu.roll(packed, 128 - k * heads, 1)

    def combine(rb):
        places = []
        owners = []
        for n in range(entries):
            owner = own_id(n) // PER_SHARD
            rank = jnp.int32(0)
            for earlier in owners:
                rank = rank + jnp.where(earlier == owner, 1, 0)
            owners.append(owner)
            places.append((jnp.clip(owner, 0, n_d - 1), jnp.minimum(rank, SLOTS - 1)))
        for u in range(spans):
            (oa, ka), (ob, kb) = places[2 * u], places[2 * u + 1]
            half_rows = pl.ds(rb * cut, cut)
            sa, sb = stat[oa, ka, half_rows], stat[ob, kb, half_rows]
            peak = jnp.maximum(sa, sb)
            ea = jnp.exp2(sa - peak)
            eb = jnp.exp2(sb - peak)
            inv = 1.0 / (ea + eb)
            ea, eb = ea * inv, eb * inv
            va, vb = orecv_half[rb][oa, ka], orecv_half[rb][ob, kb]
            for h in range(heads):
                hs = slice(h * DH, (h + 1) * DH)
                o = va[:, hs].astype(jnp.float32) * ea[:, h:h + 1] + vb[:, hs].astype(jnp.float32) * eb[:, h:h + 1]
                co[rb * rb_rows + u * cut:rb * rb_rows + (u + 1) * cut, hs] = o.astype(jnp.bfloat16)

    half_w = terms.shape[2]

    def project(rho, side, rb):
        j = ((x + rho) % n_x - d + n_d) % n_d
        block = wg[:, j, :, side * half_w:(side + 1) * half_w].reshape(width, half_w)
        return jnp.dot(co[rb * rb_rows:(rb + 1) * rb_rows], block, preferred_element_type=jnp.float32)


    def ring_copy(side, step, rb):
        rs = pl.ds(rb * rb_rows, rb_rows)
        return remote(
            xsend.at[side, step, rs], xrecv.at[side, step, rs], xs.at[side, step, rb], xr.at[side, step, rb],
            tp=(right, left)[side],
        )

    def rho_of(side, step):
        return (n_x - 1 - step) % n_x if side == 0 else (1 + step) % n_x

    def ring_start(rb):
        rs = slice(rb * rb_rows, (rb + 1) * rb_rows)
        for side in (0, 1):
            xsend[side, 0, rs] = project(rho_of(side, 0), side, rb).astype(jnp.bfloat16)
            ring_copy(side, 0, rb).start()
        for step in range(1, n_x):
            for side in (0, 1):
                terms[side * (n_x - 1) + step - 1, rs] = project(rho_of(side, step), side, rb)

    def ring_step(step, rb):
        rs = slice(rb * rb_rows, (rb + 1) * rb_rows)
        for side in (0, 1):
            ring_copy(side, step - 1, rb).wait_recv()
            total = xrecv[side, step - 1, rs].astype(jnp.float32) + terms[side * (n_x - 1) + step - 1, rs]
            xsend[side, step, rs] = total.astype(jnp.bfloat16)
            ring_copy(side, step, rb).start()

    def z_copy(rb):
        rs = pl.ds(rb * rb_rows, rb_rows)
        return remote(zsend.at[rs], zrecv.at[rs], zs.at[rb], zr.at[rb], tp=across)

    def span_rows(u, rb):
        return slice(u * SPAN + rb * cut, u * SPAN + (rb + 1) * cut)

    def ring_end(rb):
        rs = slice(rb * rb_rows, (rb + 1) * rb_rows)
        sums = []
        for side in (0, 1):
            ring_copy(side, n_x - 2, rb).wait_recv()
            sums.append(xrecv[side, n_x - 2, rs].astype(jnp.float32) + terms[side * (n_x - 1) + n_x - 2, rs])
        zsend[rs] = jnp.where(zh == 0, sums[1], sums[0]).astype(jnp.bfloat16)
        z_copy(rb).start()
        before = jnp.concatenate([hid[span_rows(u, rb)] for u in range(spans)], axis=0)
        mine[rs] = jnp.where(zh == 0, sums[0], sums[1]) + before.astype(jnp.float32)

    def finish_self():
        for h in range(heads):
            hs = slice(h * DH, (h + 1) * DH)
            att_ref[:, hs] = (acc[h] / lref[h]).astype(jnp.bfloat16)

    for n in (3, 4):
        local[n].wait()
    serve(own_q, lookups(own_id), [ref.at[d] for ref in orecv_half], strecv.at[d])
    for j in range(1, n_d):
        remote(nbv.at[0], nbv.at[j], ns.at[j], nr.at[j], db=d).wait_recv()
        id_move(j).start()
    for n in (0, 1, 2):
        local[n].wait()
    attend_first()
    for j in range(1, n_d):
        id_move(j).wait()
    weight_step(0)
    kv_start(1)
    query_step(0)
    serve_step(0)
    weight_step(1)
    query_step(1)
    serve_step(1)
    later_half(0)
    weight_step(2)
    query_step(2)
    serve_step(2)
    later_half(1)
    later_half(2)
    weight_step(3)
    advance(0, 0, 1)
    pl.when(c == 1)(lambda: wait_passed(y))
    pl.when(c == 1)(lambda: attend(i - 1, 1))
    attend_step(0)
    advance(1, 0)
    weight_step(4)
    for owner in range(n_d):
        collect(owner, 0)
    combine(0)
    weight_ready()
    local[5].wait()
    ring_start(0)
    advance(1, 1)
    for owner in range(n_d):
        collect(owner, 1)
    combine(1)
    ring_step(1, 0)
    ring_start(1)
    attend_step(1)
    ring_step(2, 0)
    ring_step(1, 1)
    local[6].wait()
    ring_end(0)
    advance(2, 0, 1)
    ring_step(2, 1)
    attend_step(2)
    ring_end(1)
    advance(3, 0, 1)
    attend_step(3)
    finish_self()
    for rb in range(ROW_BLOCKS):
        rs = slice(rb * rb_rows, (rb + 1) * rb_rows)
        z_copy(rb).wait_recv()
        whole = (mine[rs] + zrecv[rs].astype(jnp.float32)).astype(jnp.bfloat16)
        for u in range(spans):
            mixed_ref[span_rows(u, rb)] = whole[u * cut:(u + 1) * cut]

    for m in range(1, n_d):
        id_copy(m).wait_send()
        weight_copy(m).wait_send()
    for side in (0, 1):
        for hop in range(hops):
            pl.when(query_goes(side, hop))(lambda side=side, hop=hop: query_copy(side, hop).wait_send())
            pl.when(there(side, hop))(lambda side=side, hop=hop: [out_copy(side, hop, rb).wait_send() for rb in range(ROW_BLOCKS)] and None)
            pl.when(there(side, hop))(lambda side=side, hop=hop: stat_copy(side, hop).wait_send())
    for step in range(half):
        for part in (0, 1):
            if plus_has(step, part):
                pl.when(jnp.logical_and(y - step >= 0, y < n_y - 1))(
                    lambda step=step, part=part: plus_copy(step, part).wait_send())
            if minus_has(step, part):
                pl.when(minus_good((y + step) % n_y, part))(
                    lambda step=step, part=part: minus_copy(step, part).wait_send())
        wplus(step).wait_send()
        if step < half - 1:
            wminus(step).wait_send()
    for source in range(n_y):
        for part in (0, 1):
            pl.when(source < y)(lambda source=source, part=part: pass_copy(source, part, False).wait_send())
        wpass(source).wait_send()
    for part in (0, 1):
        pl.when(c == 0)(lambda part=part: pass_copy(y, part, True).wait_send())
    for side in (0, 1):
        for step in range(n_x - 1):
            for rb in range(ROW_BLOCKS):
                ring_copy(side, step, rb).wait_send()
    for rb in range(ROW_BLOCKS):
        z_copy(rb).wait_send()


def hand_over(a_ref, b_ref, a_out, b_out, sem):
    copies = [pltpu.make_async_copy(a_ref, a_out, sem.at[0]), pltpu.make_async_copy(b_ref, b_out, sem.at[1])]
    for copy in copies:
        copy.start()
    for copy in copies:
        copy.wait()


def shards(sizes, hidden_in, queries, keys, values, cross_queries, neighbours, database, out_weight):
    n_y, n_d, n_x = sizes
    half = n_y // 2
    rows, width = queries.shape[1:]
    heads = width // DH
    spans = rows // SPAN
    n_c = 2 * n_y
    piece = width // n_c
    cols = out_weight.shape[1]
    half_w = cols // 2
    bf16, f32 = jnp.bfloat16, jnp.float32
    vm, dma = pltpu.VMEM, pltpu.SemaphoreType.DMA
    any_spec = pl.BlockSpec(memory_space=pl.ANY)
    scratch = [vm((spans, SPAN, width), bf16) for _ in range(2 * n_d - 1)] + [
        vm((n_c, 2, rows, width), bf16),
        vm((rows, width), bf16),
        vm((rows, width), bf16),
        pltpu.SMEM((spans, NEIGH), jnp.int32),
        vm((n_d, 8, 128), jnp.int32),
        pltpu.SMEM((n_d, 8, 128), jnp.int32),
        vm(database.shape, bf16),
        vm((n_c, n_d, piece, cols), bf16),
        vm((2, n_d - 1, ROW_BLOCKS, SLOTS, SPAN // ROW_BLOCKS, width), bf16),
        vm((n_d, SLOTS, SPAN // ROW_BLOCKS, width), bf16),
        vm((n_d, SLOTS, SPAN // ROW_BLOCKS, width), bf16),
        vm((2, n_d - 1, SPAN, 128), f32),
        vm((n_d, SPAN, 128), f32),
        vm((n_d, SLOTS, SPAN, 128), f32),
        vm((rows, width), bf16),
        vm((2 * (n_x - 1), rows, half_w), f32),
        vm((2, n_x - 1, rows, half_w), bf16),
        vm((2, n_x - 1, rows, half_w), bf16),
        vm((rows, half_w), f32),
        vm((rows, half_w), bf16),
        vm((rows, half_w), bf16),
        vm((heads, rows, 1), f32),
        vm((heads, rows, 1), f32),
        vm((heads, rows, DH), f32),
        dma((8,)),
        dma((half, 2)), dma((half, 2)), dma((half, 2)), dma((half, 2)),
        dma((n_y, 2)), dma((n_y, 2)),
        dma((2, n_d - 1)), dma((2, n_d - 1)), dma((n_d,)), dma((n_d,)), dma((n_d,)),
        dma((2, n_d - 1, ROW_BLOCKS)), dma((n_d, ROW_BLOCKS)), dma((2, n_d - 1)), dma((n_d,)),
        dma((n_d,)), dma((n_d,)),
        dma((half,)), dma((half,)), dma((half,)), dma((half,)),
        dma((n_y,)), dma((n_y,)),
        dma((2, n_x - 1, ROW_BLOCKS)), dma((2, n_x - 1, ROW_BLOCKS)),
        dma((ROW_BLOCKS,)), dma((ROW_BLOCKS,)),
    ]
    attended, mixed = pl.pallas_call(
        functools.partial(layer, sizes),
        out_shape=(
            jax.ShapeDtypeStruct((rows, width), bf16),
            jax.ShapeDtypeStruct((rows, half_w), bf16),
        ),
        in_specs=[any_spec] * 8,
        out_specs=(pl.BlockSpec(memory_space=pltpu.VMEM), pl.BlockSpec(memory_space=pltpu.VMEM)),
        scratch_shapes=scratch,
        compiler_params=pltpu.CompilerParams(
            collective_id=0, has_side_effects=True, vmem_limit_bytes=56 * 1024 * 1024
        ),
        name="layer",
    )(
        neighbours,
        hidden_in[0],
        queries[0],
        keys[0],
        values[0],
        cross_queries[0].reshape(spans, SPAN, width),
        database,
        out_weight.reshape(n_c, piece, cols),
    )
    attended, mixed = pl.pallas_call(
        hand_over,
        out_shape=(
            jax.ShapeDtypeStruct((rows, width), bf16),
            jax.ShapeDtypeStruct((rows, half_w), bf16),
        ),
        in_specs=[pl.BlockSpec(memory_space=pltpu.VMEM)] * 2,
        out_specs=(any_spec, any_spec),
        scratch_shapes=[dma((2,))],
        name="hand_over",
    )(attended, mixed)
    return attended[None], mixed[None]


def solution(mesh):
    sizes = (mesh.shape["ctx"] // 2, mesh.shape["db"], mesh.shape["tp"] // 2)
    in_specs = (
        P("db", "ctx", "tp"),
        P("db", "ctx", "tp"),
        P("db", "ctx", "tp"),
        P("db", "ctx", "tp"),
        P("db", "ctx", "tp"),
        P("db", "ctx", None),
        P(None, "db", None, "tp"),
        P("tp", "db"),
    )
    out_specs = (P("db", "ctx", "tp"), P("db", "ctx", "tp"))
    return jax.shard_map(
        functools.partial(shards, sizes), mesh=mesh, in_specs=in_specs, out_specs=out_specs, check_vma=False
    )
```
